128 devices in a mesh: parts: 128 (over y, z, x, core).
Axes of the slice: x: 4, y: 4, z: 4, core: 2. Of those that a mesh axis runs over, the one named last changes fastest.
Arguments:
- rhs: float32 [4, 131072], P(None, 'parts'), may hold values from -6 to 6
- diag_tiles: bfloat16 [1024, 512, 512], P('parts'), may hold values from -1 to 6, as said below
- local_tiles: bfloat16 [1024, 3, 512, 512], P('parts'), may hold values from -0.125 to 0.125
- up_tiles: bfloat16 [384, 512, 512], P('parts'), may hold values from -0.375 to 0.375
- down_tiles: bfloat16 [384, 512, 512], P('parts'), may hold values from -0.375 to 0.375
- pattern: int32 [1024, 3], P('parts'), may hold values from 0 to 7
- coupling_rows: int32 [128, 6], P('parts'), may hold values from 0 to 7
- ghost_rows: int32 [128, 6, 128], P('parts'), may hold values from 0 to 1023
- pair_live: int32 [128, 3], P('parts'), may hold values 0 or 1
Outputs:
- adjoint: float32 [4, 131072], P(None, 'parts')
The draws below stay inside these ranges and needn't reach their ends.
Inputs may be any that keep to these rules, and one draw needn't show every extreme that they name: `diag_tiles`: each tile is its own diagonal entries of 0.5 to 5 plus a dense remainder of smaller entries.
All inputs are finite; a program needn't handle non-finite values. No bound on the sum of `pair_live` on one device may be relied on, other than what follows from the above.
Results may differ from the reference program's by a relative error of at most 0.0028.
Values may be sent and summed in bfloat16 or wider, within the bound.
A program may use at most 128 MiB of HBM per device.

```python
import math
import jax
import jax.numpy as jnp
from jax import lax

COMP = 4
TILE = 128
TD = 8
KL = 3
W = 3
ITERS = 3
NODES = 131072
N_PARTS = 128


def draw_diag_tiles(key, part):
    width = COMP * TILE
    first, second, third = jax.random.split(key, 3)
    rest = jax.random.normal(first, (N_PARTS * TD, width, width), jnp.float32)
    level = jnp.exp(jax.random.uniform(second, (N_PARTS, 1), jnp.float32, math.log(0.5), math.log(2.0)))
    factor = jnp.exp(jax.random.uniform(third, (N_PARTS, TD * width), jnp.float32, 0.0, math.log(2.5)))
    rest = rest / (4.0 * width ** 0.5)
    shift = (level * factor).reshape(N_PARTS * TD, width)
    return (rest + shift[:, :, None] * jnp.eye(width, dtype=jnp.float32)[None, :, :]).astype(jnp.bfloat16)


def plant(values, rng, least, largest):
    place = [jax.random.randint(jax.random.fold_in(rng, axis), (), 0, length) for axis, length in enumerate(values.shape)]
    main_axis = values.shape.index(max(values.shape))
    beside = place[:main_axis] + [(place[main_axis] + 1) % values.shape[main_axis]] + place[main_axis + 1:]
    return values.at[tuple(place)].set(least).at[tuple(beside)].set(largest)


def shard_levels(key, shape, shards, smallest, high):
    def one(position, shards_of):
        draws = jax.random.uniform(jax.random.fold_in(jax.random.fold_in(key, 6), position), (shards_of,), jnp.float32, smallest / len(shards), high / len(shards))
        return jnp.repeat(jnp.exp(draws), shape[position] // shards_of).reshape((-1,) + (1,) * (len(shape) - position - 1))

    gain = one(*shards[0])
    for cut in shards[1:]:
        gain = gain * one(*cut)
    return gain


def noise(own_key, shape, spread, reach, pieces=(), kind=jnp.bfloat16):
    level = shard_levels(own_key, shape, pieces, -0.22, 0.18) if pieces else 1.0
    values = jax.random.normal(own_key, shape, jnp.float32) * spread * level
    return jnp.minimum(jnp.maximum(values, -reach), reach).astype(kind)


def setup_inputs(seed: int = 0) -> dict:
    splits = jax.random.split(jax.random.key(seed), 10)
    rhs = noise(splits[0], (COMP, NODES), 1.0, 6.0, ((1, 128),), jnp.float32)
    diag_tiles = draw_diag_tiles(jax.random.fold_in(splits[9], 71), 0)
    local_tiles = noise(splits[2], (N_PARTS * TD, KL, COMP * TILE, COMP * TILE), (4 * COMP * TILE) ** -0.5, 0.125, ((0, 128),))
    up_tiles = noise(splits[3], (N_PARTS * W, COMP * TILE, COMP * TILE), (COMP * TILE // 2) ** -0.5, 0.375, ((0, 128),))
    down_tiles = noise(splits[4], (N_PARTS * W, COMP * TILE, COMP * TILE), (COMP * TILE // 2) ** -0.5, 0.375, ((0, 128),))
    pattern = plant(jax.random.randint(splits[5], (N_PARTS * TD, KL), 0, TD), jax.random.fold_in(splits[5], 1), 0, TD - 1).astype(jnp.int32)
    coupling_rows = plant(jax.random.randint(splits[6], (N_PARTS, 2 * W), 0, TD), jax.random.fold_in(splits[6], 1), 0, TD - 1).astype(jnp.int32)
    ghost_rows = plant(jax.random.randint(splits[7], (N_PARTS, 2 * W, TILE), 0, TD * TILE), jax.random.fold_in(splits[7], 1), 0, (TD * TILE) - 1).astype(jnp.int32)
    pair_live = plant((jax.random.randint(splits[8], (N_PARTS, W), 0, 4) < 3).astype(jnp.int32), jax.random.fold_in(splits[8], 1), 0, 1)
    return {"rhs": rhs, "diag_tiles": diag_tiles, "local_tiles": local_tiles, "up_tiles": up_tiles, "down_tiles": down_tiles, "pattern": pattern, "coupling_rows": coupling_rows, "ghost_rows": ghost_rows, "pair_live": pair_live}


def tile_view(vec):
    return vec.reshape(COMP, N_PARTS, TD, TILE).transpose(1, 2, 0, 3).reshape(N_PARTS, TD, COMP * TILE)

def node_view(tiles):
    return tiles.reshape(N_PARTS, TD, COMP, TILE).transpose(2, 0, 1, 3).reshape(COMP, NODES)

def adjoint_apply(vec, diag_tiles, local_tiles, up_tiles, down_tiles, pattern, coupling_rows, ghost_rows, pair_live):
    width = COMP * TILE
    rounded = tile_view(vec).astype(jnp.bfloat16)
    diag_all = diag_tiles.reshape(N_PARTS, TD, width, width)
    local_all = local_tiles.reshape(N_PARTS, TD, KL, width, width)
    up_all = up_tiles.reshape(N_PARTS, W, width, width)
    down_all = down_tiles.reshape(N_PARTS, W, width, width)
    pattern_all = pattern.reshape(N_PARTS, TD, KL)

    def part_fn(item):
        diag_p, local_p, up_p, down_p, pat_p, rows_p, tiles_p = item
        vals = tiles_p.astype(jnp.float32)
        own = jnp.einsum('tr,trc->tc', vals, diag_p.astype(jnp.float32))
        mixed = jnp.einsum('tr,tkrc->tkc', vals, local_p.astype(jnp.float32))
        onehot = (pat_p[:, :, None] == jnp.arange(TD, dtype=jnp.int32)[None, None, :]).astype(jnp.float32)
        own = own + jnp.einsum('tkj,tkc->jc', onehot, mixed)
        up_terms = jnp.einsum('wr,wrc->wc', vals[rows_p[:W]], up_p.astype(jnp.float32))
        down_terms = jnp.einsum('wr,wrc->wc', vals[rows_p[W:]], down_p.astype(jnp.float32))
        return (own, up_terms, down_terms)
    own, up_terms, down_terms = lax.map(part_fn, (diag_all, local_all, up_all, down_all, pattern_all, coupling_rows, rounded))
    live = pair_live.astype(jnp.float32)
    part_ids = jnp.arange(N_PARTS, dtype=jnp.int32)
    offsets = jnp.arange(1, W + 1, dtype=jnp.int32)
    slots = jnp.arange(W, dtype=jnp.int32)
    lower = (part_ids[:, None] - offsets[None, :]) % N_PARTS
    upper = (part_ids[:, None] + offsets[None, :]) % N_PARTS
    live_down = live[lower, slots[None, :]]
    up_terms = up_terms * live[:, :, None]
    down_terms = down_terms * live_down[:, :, None]
    up_index = (upper * (TD * TILE))[:, :, None] + ghost_rows[:, :W, :]
    down_index = (lower * (TD * TILE))[:, :, None] + ghost_rows[:, W:, :]
    result = node_view(own)
    up_vals = up_terms.reshape(N_PARTS, W, COMP, TILE).transpose(2, 0, 1, 3).reshape(COMP, N_PARTS * W * TILE)
    down_vals = down_terms.reshape(N_PARTS, W, COMP, TILE).transpose(2, 0, 1, 3).reshape(COMP, N_PARTS * W * TILE)
    result = result.at[:, up_index.reshape(-1)].add(up_vals)
    result = result.at[:, down_index.reshape(-1)].add(down_vals)
    return result

def reference(rhs, diag_tiles, local_tiles, up_tiles, down_tiles, pattern, coupling_rows, ghost_rows, pair_live):
    beta = jnp.sqrt(jnp.sum(rhs * rhs) + 1e-06)
    basis = [rhs / beta]
    hess = jnp.zeros((ITERS + 1, ITERS), jnp.float32)
    for j in range(ITERS):
        vector = adjoint_apply(basis[j], diag_tiles, local_tiles, up_tiles, down_tiles, pattern, coupling_rows, ghost_rows, pair_live)
        for i in range(j + 1):
            coeff = jnp.sum(vector * basis[i])
            hess = hess.at[i, j].set(coeff)
            vector = vector - coeff * basis[i]
        scale = jnp.sqrt(jnp.sum(vector * vector) + 1e-06)
        hess = hess.at[j + 1, j].set(scale)
        basis.append(vector / scale)
    gram = jnp.dot(hess.T, hess, precision=lax.Precision.HIGHEST)
    target = beta * hess[0, :]
    factor = jnp.linalg.cholesky(gram)
    inner = lax.linalg.triangular_solve(factor, target[:, None], left_side=True, lower=True)
    coeffs = lax.linalg.triangular_solve(factor, inner, left_side=True, lower=True, transpose_a=True)[:, 0]
    adjoint = jnp.zeros_like(rhs)
    for j in range(ITERS):
        adjoint = adjoint + coeffs[j] * basis[j]
    return adjoint
```

```python
import functools

import jax
import jax.numpy as jnp
from jax import lax
from jax.experimental import pallas as pl
from jax.experimental.pallas import tpu as pltpu
from jax.sharding import PartitionSpec as P

COMP = 4
TILE = 128
TD = 8
KL = 3
W = 3
ITERS = 3
WIDTH = COMP * TILE
SLOTS = 2 * W
PER_ROW = KL + 1
SHIFT = 2.0
EPS = 1e-06
ROW = 8
MESH = pl.DeviceIdType.MESH
F32 = jnp.float32
BF16 = jnp.bfloat16
PAIRS = [(i, j) for i in range(ITERS + 1) for j in range(i, ITERS + 1)]


def lanes(c):
    return slice(c * TILE, (c + 1) * TILE)


def halves(x):
    high = x.astype(BF16).astype(F32)
    return jnp.concatenate([high, x - high], axis=0).astype(BF16)


def small_solve(gram):
    n = ITERS + 1

    def g(i, j):
        return gram[(min(i, j), max(i, j))]

    def dot(u, v):
        total = None
        for i, a in u.items():
            for j, b in v.items():
                term = a * b * g(i, j)
                total = term if total is None else total + term
        return total

    beta = jnp.sqrt(g(0, 0) + EPS)
    basis = [{0: 1.0 / beta}]
    hess = {}
    for j in range(ITERS):
        w = {}
        for i, a in basis[j].items():
            w[i + 1] = a + w[i + 1] if i + 1 in w else a
            w[i] = SHIFT * a + w[i] if i in w else SHIFT * a
        for i in range(j + 1):
            hess[i, j] = dot(w, basis[i])
            for k, b in basis[i].items():
                w[k] = w[k] - hess[i, j] * b
        scale = jnp.sqrt(jnp.maximum(dot(w, w), 0.0) + EPS)
        hess[j + 1, j] = scale
        if j + 1 < ITERS:
            inverse = 1.0 / scale
            basis.append({k: a * inverse for k, a in w.items()})
    normal = {}
    for a in range(ITERS):
        for b in range(a + 1):
            normal[a, b] = sum(
                hess[i, a] * hess[i, b] for i in range(n) if (i, a) in hess and (i, b) in hess
            )
    target = [beta * hess[0, j] for j in range(ITERS)]
    low = {}
    inv = []
    for a in range(ITERS):
        for b in range(a):
            value = normal[a, b]
            for k in range(b):
                value = value - low[a, k] * low[b, k]
            low[a, b] = value * inv[b]
        value = normal[a, a]
        for k in range(a):
            value = value - low[a, k] * low[a, k]
        inv.append(1.0 / jnp.sqrt(value))
    inner = []
    for a in range(ITERS):
        value = target[a]
        for k in range(a):
            value = value - low[a, k] * inner[k]
        inner.append(value * inv[a])
    weights = [None] * ITERS
    for a in reversed(range(ITERS)):
        value = inner[a]
        for k in range(a + 1, ITERS):
            value = value - low[k, a] * weights[k]
        weights[a] = value * inv[a]
    out = []
    for i in range(ITERS):
        out.append(sum(weights[j] * basis[j][i] for j in range(ITERS) if i in basis[j]))
    return out


def kernel(
    n,
    rhs_hbm,
    diag_hbm,
    local_hbm,
    up_hbm,
    down_hbm,
    pattern,
    rows,
    ghost_hbm,
    live,
    out_ref,
    tiles,
    rhs,
    krylov,
    nodes,
    spread,
    masks,
    ghosts,
    pick,
    place,
    sent,
    got,
    part_a,
    part_b,
    recv_a,
    recv_b,
    load_sem,
    ghost_send,
    ghost_recv,
    halo_send,
    halo_recv,
    send_a,
    got_a,
    send_b,
    got_b,
):
    me = lax.axis_index("parts")
    columns = n // ROW
    place_in_row = lax.rem(me, ROW)
    base = me - place_in_row
    around = [lax.rem(me + s + 1, n) for s in range(W)] + [
        lax.rem(me + n - s - 1, n) for s in range(W)
    ]
    peers_a = [base + lax.rem(place_in_row + d, ROW) for d in range(1, ROW)]
    peers_b = [lax.rem(me + d * ROW, n) for d in range(1, columns)]
    everyone = around + peers_a + peers_b
    barrier = pltpu.get_barrier_semaphore()
    for other in everyone:
        pl.semaphore_signal(barrier, inc=1, device_id=(other,), device_id_type=MESH)

    loads = []

    def load(source, target):
        copy = pltpu.make_async_copy(source, target, load_sem.at[len(loads)])
        copy.start()
        loads.append(copy)
        return copy

    load_rhs = load(rhs_hbm, rhs)
    load_up = load(up_hbm, tiles.at[pl.ds(0, W)])
    load_down = load(down_hbm, tiles.at[pl.ds(W, W)])
    load_rows = []
    for t in range(TD):
        first = SLOTS + PER_ROW * t
        load_rows.append(
            (
                load(diag_hbm.at[t], tiles.at[first]),
                load(local_hbm.at[t], tiles.at[pl.ds(first + 1, KL)]),
            )
        )

    pl.semaphore_wait(barrier, len(everyone))
    ghost_copies = []
    for s in range(SLOTS):
        copy = pltpu.make_async_remote_copy(
            src_ref=ghost_hbm.at[0, pl.ds(s, 1)],
            dst_ref=ghosts.at[s],
            send_sem=ghost_send.at[s],
            recv_sem=ghost_recv.at[s],
            device_id=(around[s],),
            device_id_type=MESH,
        )
        copy.start()
        ghost_copies.append(copy)

    sub16 = lax.rem(lax.broadcasted_iota(jnp.int32, (2 * TD, TILE), 0), TD)
    sub8 = lax.broadcasted_iota(jnp.int32, (TD, TILE), 0)
    for t in range(TD):
        for k in range(KL):
            masks[KL * t + k] = jnp.where(sub16 == pattern[t, k], 1.0, 0.0).astype(BF16)

    load_rhs.wait()
    for t in range(TD):
        for c in range(COMP):
            krylov[0, t : t + 1, lanes(c)] = rhs[c : c + 1, lanes(t)]

    def spread_vector(j):
        for t in range(TD):
            row = jnp.broadcast_to(krylov[j, t : t + 1, :], (TD, WIDTH))
            spread[t] = halves(row)

    def send_couplings(j):
        copies = []
        for s in range(SLOTS):
            left = spread[rows[0, s]]
            both = jnp.dot(left, tiles[s], preferred_element_type=F32)
            term = both[:TD] + both[TD:]
            message = jnp.where(sub8 == 0, term[:, lanes(0)], 0.0)
            for c in range(1, COMP):
                message = jnp.where(sub8 == c, term[:, lanes(c)], message)
            if s < W:
                message = message * live[0, s].astype(F32)
            sent[j, s] = message
            copy = pltpu.make_async_remote_copy(
                src_ref=sent.at[j, s],
                dst_ref=got.at[j, s],
                send_sem=halo_send.at[j, s],
                recv_sem=halo_recv.at[j, s],
                device_id=(around[s],),
                device_id_type=MESH,
            )
            copy.start()
            copies.append(copy)
        return copies

    def multiply_own(j):
        total = None
        for t in range(TD):
            if j == 0:
                for copy in load_rows[t]:
                    copy.wait()
            vector = spread[t]
            for k in range(PER_ROW):
                if k == 0:
                    mask = jnp.where(sub16 == t, 1.0, 0.0).astype(BF16)
                else:
                    mask = masks[KL * t + k - 1]
                left = vector * jnp.concatenate([mask] * COMP, axis=1)
                part = jnp.dot(left, tiles[SLOTS + PER_ROW * t + k], preferred_element_type=F32)
                total = part if total is None else total + part
        return total[:TD] + total[TD:]

    def finish(j, own, copies):
        for copy in copies:
            copy.wait_recv()
        left = []
        for c in range(COMP):
            blocks = []
            for s in range(SLOTS):
                row = jnp.broadcast_to(got[j, s, c : c + 1, :], (TD, TILE))
                blocks.append(halves(row) * place[s])
            left.append(jnp.concatenate(blocks, axis=1))
        added = jnp.dot(jnp.concatenate(left, axis=0), pick[...], preferred_element_type=F32)
        for c in range(COMP):
            first = 2 * TD * c
            krylov[j + 1, :, lanes(c)] = (
                own[:, lanes(c)]
                + (added[first : first + TD] + added[first + TD : first + 2 * TD])
                - SHIFT * krylov[j, :, lanes(c)]
            )

    def pair_row(i, j):
        total = None
        for c in range(COMP):
            term = krylov[i, :, lanes(c)] * krylov[j, :, lanes(c)]
            total = term if total is None else total + term
        return jnp.sum(total, axis=0, keepdims=True)

    all_copies = list(ghost_copies)
    for j in range(ITERS):
        spread_vector(j)
        if j == 0:
            load_up.wait()
            load_down.wait()
        copies = send_couplings(j)
        all_copies.extend(copies)
        if j == 0:
            for s in range(SLOTS):
                ghost_copies[s].wait_recv()
                index = jnp.broadcast_to(ghosts[s], (TILE, TILE))
                sub = lax.broadcasted_iota(jnp.int32, (TILE, TILE), 0)
                chosen = jnp.where(jnp.bitwise_and(index, TILE - 1) == sub, 1.0, 0.0)
                pick[s * TILE : (s + 1) * TILE, :] = chosen.T.astype(BF16)
                row = jnp.broadcast_to(ghosts[s], (2 * TD, TILE))
                where = jnp.where(jnp.right_shift(row, 7) == sub16, 1.0, 0.0)
                if s >= W:
                    where = where * live[0, s - W].astype(F32)
                place[s] = where.astype(BF16)
        own = multiply_own(j)
        finish(j, own, copies)

    total = jnp.zeros((2 * TD, TILE), F32)
    sub = lax.broadcasted_iota(jnp.int32, (2 * TD, TILE), 0)
    for position, (i, j) in enumerate(PAIRS):
        total = jnp.where(sub == position, pair_row(i, j), total)
    part_a[...] = total
    stage_a = []
    for d in range(1, ROW):
        copy = pltpu.make_async_remote_copy(
            src_ref=part_a,
            dst_ref=recv_a.at[d - 1],
            send_sem=send_a.at[d - 1],
            recv_sem=got_a.at[d - 1],
            device_id=(peers_a[d - 1],),
            device_id_type=MESH,
        )
        copy.start()
        stage_a.append(copy)
    for j in range(1, ITERS):
        for t in range(TD):
            for c in range(COMP):
                nodes[j - 1, c : c + 1, lanes(t)] = krylov[j, t : t + 1, lanes(c)]
    for copy in stage_a:
        copy.wait_recv()
    for d in range(1, ROW):
        total = total + recv_a[d - 1]
    part_b[...] = total
    stage_b = []
    for d in range(1, columns):
        copy = pltpu.make_async_remote_copy(
            src_ref=part_b,
            dst_ref=recv_b.at[d - 1],
            send_sem=send_b.at[d - 1],
            recv_sem=got_b.at[d - 1],
            device_id=(peers_b[d - 1],),
            device_id_type=MESH,
        )
        copy.start()
        stage_b.append(copy)
    for copy in stage_b:
        copy.wait_recv()
    for d in range(1, columns):
        total = total + recv_b[d - 1]
    sums = jnp.sum(total, axis=1, keepdims=True)
    gram = {
        pair: jnp.broadcast_to(sums[position : position + 1, :], (TD, TILE))
        for position, pair in enumerate(PAIRS)
    }
    weights = [weight[:COMP] for weight in small_solve(gram)]
    for t in range(TD):
        value = weights[0] * rhs[:, lanes(t)]
        for j in range(1, ITERS):
            value = value + weights[j] * nodes[j - 1, :, lanes(t)]
        out_ref[:, lanes(t)] = value
    for copy in all_copies + stage_a + stage_b:
        copy.wait_send()


def local(n, *arrays):
    anywhere = pl.BlockSpec(memory_space=pl.ANY)
    scalars = pl.BlockSpec(memory_space=pltpu.SMEM)
    vmem = pltpu.VMEM
    dma = pltpu.SemaphoreType.DMA
    columns = n // ROW
    rhs = arrays[0]
    return pl.pallas_call(
        functools.partial(kernel, n),
        out_shape=jax.ShapeDtypeStruct(rhs.shape, F32),
        in_specs=[anywhere] * 5 + [scalars] * 2 + [anywhere, scalars],
        out_specs=pl.BlockSpec(memory_space=pltpu.VMEM),
        scratch_shapes=[
            vmem((SLOTS + PER_ROW * TD, WIDTH, WIDTH), BF16),
            vmem(rhs.shape, F32),
            vmem((ITERS + 1, TD, WIDTH), F32),
            vmem((ITERS - 1,) + rhs.shape, F32),
            vmem((TD, 2 * TD, WIDTH), BF16),
            vmem((TD * KL, 2 * TD, TILE), BF16),
            vmem((SLOTS, 1, TILE), jnp.int32),
            vmem((SLOTS * TILE, TILE), BF16),
            vmem((SLOTS, 2 * TD, TILE), BF16),
            vmem((ITERS, SLOTS, TD, TILE), F32),
            vmem((ITERS, SLOTS, TD, TILE), F32),
            vmem((2 * TD, TILE), F32),
            vmem((2 * TD, TILE), F32),
            vmem((ROW - 1, 2 * TD, TILE), F32),
            vmem((columns - 1, 2 * TD, TILE), F32),
            dma((3 + 2 * TD,)),
            dma((SLOTS,)),
            dma((SLOTS,)),
            dma((ITERS, SLOTS)),
            dma((ITERS, SLOTS)),
            dma((ROW - 1,)),
            dma((ROW - 1,)),
            dma((columns - 1,)),
            dma((columns - 1,)),
        ],
        compiler_params=pltpu.CompilerParams(
            collective_id=0, has_side_effects=True, vmem_limit_bytes=48 << 20
        ),
    )(*arrays)


def solution(mesh):
    in_specs = (
        P(None, "parts"),
        P("parts", None, None),
        P("parts", None, None, None),
        P("parts", None, None),
        P("parts", None, None),
        P("parts", None),
        P("parts", None),
        P("parts", None, None),
        P("parts", None),
    )
    return jax.shard_map(
        functools.partial(local, mesh.shape["parts"]),
        mesh=mesh,
        in_specs=in_specs,
        out_specs=P(None, "parts"),
        check_vma=False,
    )
```

```python
import functools
import itertools

import jax
import jax.numpy as jnp
from jax import lax
from jax.experimental import pallas as pl
from jax.experimental.pallas import tpu as pltpu
from jax.sharding import PartitionSpec as P

COMP = 4
TILE = 128
TD = 8
KL = 3
W = 3
ITERS = 3
WIDTH = COMP * TILE
SLOTS = 2 * W
PER_ROW = KL + 1
SHIFT = 2.0
EPS = 1e-06
MESH = pl.DeviceIdType.MESH
F32 = jnp.float32
BF16 = jnp.bfloat16
SIDE = 4
OFFSETS = sorted(
    itertools.product(range(SIDE), repeat=3), key=lambda d: -sum(min(k, SIDE - k) for k in d)
)[:-1]
PAIRS = [(i, j) for i in range(ITERS + 1) for j in range(i, ITERS + 1)]


def lanes(c):
    return slice(c * TILE, (c + 1) * TILE)


def halves(x):
    high = x.astype(BF16).astype(F32)
    return jnp.concatenate([high, x - high], axis=0).astype(BF16)


def small_solve(gram):
    n = ITERS + 1

    def g(i, j):
        return gram[(min(i, j), max(i, j))]

    def dot(u, v):
        total = None
        for i, a in u.items():
            for j, b in v.items():
                term = a * b * g(i, j)
                total = term if total is None else total + term
        return total

    beta = jnp.sqrt(g(0, 0) + EPS)
    basis = [{0: 1.0 / beta}]
    hess = {}
    for j in range(ITERS):
        w = {}
        for i, a in basis[j].items():
            w[i + 1] = a + w[i + 1] if i + 1 in w else a
            w[i] = SHIFT * a + w[i] if i in w else SHIFT * a
        for i in range(j + 1):
            hess[i, j] = dot(w, basis[i])
            for k, b in basis[i].items():
                w[k] = w[k] - hess[i, j] * b
        scale = jnp.sqrt(jnp.maximum(dot(w, w), 0.0) + EPS)
        hess[j + 1, j] = scale
        if j + 1 < ITERS:
            inverse = 1.0 / scale
            basis.append({k: a * inverse for k, a in w.items()})
    normal = {}
    for a in range(ITERS):
        for b in range(a + 1):
            normal[a, b] = sum(
                hess[i, a] * hess[i, b] for i in range(n) if (i, a) in hess and (i, b) in hess
            )
    target = [beta * hess[0, j] for j in range(ITERS)]
    low = {}
    inv = []
    for a in range(ITERS):
        for b in range(a):
            value = normal[a, b]
            for k in range(b):
                value = value - low[a, k] * low[b, k]
            low[a, b] = value * inv[b]
        value = normal[a, a]
        for k in range(a):
            value = value - low[a, k] * low[a, k]
        inv.append(1.0 / jnp.sqrt(value))
    inner = []
    for a in range(ITERS):
        value = target[a]
        for k in range(a):
            value = value - low[a, k] * inner[k]
        inner.append(value * inv[a])
    weights = [None] * ITERS
    for a in reversed(range(ITERS)):
        value = inner[a]
        for k in range(a + 1, ITERS):
            value = value - low[k, a] * weights[k]
        weights[a] = value * inv[a]
    out = []
    for i in range(ITERS):
        out.append(sum(weights[j] * basis[j][i] for j in range(ITERS) if i in basis[j]))
    return out


def kernel(
    n,
    rhs_hbm,
    diag_hbm,
    local_hbm,
    up_hbm,
    down_hbm,
    pattern_hbm,
    rows_hbm,
    ghost_hbm,
    live_hbm,
    out_ref,
    pattern,
    rows,
    live,
    tiles,
    rhs,
    krylov,
    nodes,
    spread,
    masks,
    ghosts,
    pick,
    place,
    sent,
    got,
    part_a,
    recv_a,
    recv_b,
    load_sem,
    ghost_send,
    ghost_recv,
    halo_send,
    halo_recv,
    send_a,
    got_a,
    send_b,
    got_b,
):
    me = lax.axis_index("parts")
    around = [lax.rem(me + s + 1, n) for s in range(W)] + [
        lax.rem(me + n - s - 1, n) for s in range(W)
    ]
    core = lax.rem(me, 2)
    digits = [lax.rem(me // 2, SIDE), lax.rem(me // (2 * SIDE), SIDE), me // (2 * SIDE * SIDE)]
    moved = [
        [2 * SIDE**axis * lax.rem(digits[axis] + d, SIDE) for d in range(SIDE)] for axis in range(3)
    ]
    partner = me + 1 - 2 * core
    chips = [core + moved[0][dx] + moved[1][dz] + moved[2][dy] for dx, dz, dy in OFFSETS]

    loads = []

    def load(source, target):
        copy = pltpu.make_async_copy(source, target, load_sem.at[len(loads)])
        copy.start()
        loads.append(copy)
        return copy

    load_rhs = load(rhs_hbm, rhs)
    load_small = [load(rows_hbm, rows), load(live_hbm, live), load(pattern_hbm, pattern)]
    load_up = load(up_hbm, tiles.at[pl.ds(0, W)])
    load_down = load(down_hbm, tiles.at[pl.ds(W, W)])
    load_rows = []
    for t in range(TD):
        first = SLOTS + PER_ROW * t
        load_rows.append(
            (
                load(diag_hbm.at[t], tiles.at[first]),
                load(local_hbm.at[t], tiles.at[pl.ds(first + 1, KL)]),
            )
        )

    everyone = around + [partner] + chips
    barrier = pltpu.get_barrier_semaphore()
    for other in everyone:
        pl.semaphore_signal(barrier, inc=1, device_id=(other,), device_id_type=MESH)

    pl.semaphore_wait(barrier, len(everyone))
    ghost_copies = []
    for s in range(SLOTS):
        copy = pltpu.make_async_remote_copy(
            src_ref=ghost_hbm.at[s],
            dst_ref=ghosts.at[s],
            send_sem=ghost_send.at[s],
            recv_sem=ghost_recv.at[s],
            device_id=(around[s],),
            device_id_type=MESH,
        )
        copy.start()
        ghost_copies.append(copy)

    for copy in load_small:
        copy.wait()
    sub16 = lax.rem(lax.broadcasted_iota(jnp.int32, (2 * TD, TILE), 0), TD)
    sub8 = lax.broadcasted_iota(jnp.int32, (TD, TILE), 0)
    for t in range(TD):
        for k in range(KL):
            masks[KL * t + k] = jnp.where(sub16 == pattern[k, t], 1.0, 0.0).astype(BF16)

    load_rhs.wait()
    for t in range(TD):
        for c in range(COMP):
            krylov[0, t : t + 1, lanes(c)] = rhs[c : c + 1, lanes(t)]

    def spread_vector(j):
        for t in range(TD):
            row = jnp.broadcast_to(krylov[j, t : t + 1, :], (TD, WIDTH))
            spread[t] = halves(row)

    def send_couplings(j):
        copies = []
        for s in range(SLOTS):
            left = spread[rows[0, s]]
            both = jnp.dot(left, tiles[s], preferred_element_type=F32)
            term = both[:TD] + both[TD:]
            message = jnp.where(sub8 == 0, term[:, lanes(0)], 0.0)
            for c in range(1, COMP):
                message = jnp.where(sub8 == c, term[:, lanes(c)], message)
            if s < W:
                message = message * live[0, s].astype(F32)
            sent[j, s] = message
            copy = pltpu.make_async_remote_copy(
                src_ref=sent.at[j, s],
                dst_ref=got.at[j, s],
                send_sem=halo_send.at[j, s],
                recv_sem=halo_recv.at[j, s],
                device_id=(around[s],),
                device_id_type=MESH,
            )
            copy.start()
            copies.append(copy)
        return copies

    def multiply_own(j):
        total = None
        for t in range(TD):
            if j == 0:
                for copy in load_rows[t]:
                    copy.wait()
            vector = spread[t]
            for k in range(PER_ROW):
                if k == 0:
                    mask = jnp.where(sub16 == t, 1.0, 0.0).astype(BF16)
                else:
                    mask = masks[KL * t + k - 1]
                left = vector * jnp.concatenate([mask] * COMP, axis=1)
                part = jnp.dot(left, tiles[SLOTS + PER_ROW * t + k], preferred_element_type=F32)
                total = part if total is None else total + part
        return total[:TD] + total[TD:]

    def finish(j, own, copies):
        for copy in copies:
            copy.wait_recv()
        left = []
        for c in range(COMP):
            blocks = []
            for s in range(SLOTS):
                row = jnp.broadcast_to(got[j, s, c : c + 1, :], (TD, TILE))
                blocks.append(halves(row) * place[s])
            left.append(jnp.concatenate(blocks, axis=1))
        added = jnp.dot(jnp.concatenate(left, axis=0), pick[...], preferred_element_type=F32)
        for c in range(COMP):
            first = 2 * TD * c
            krylov[j + 1, :, lanes(c)] = (
                own[:, lanes(c)]
                + (added[first : first + TD] + added[first + TD : first + 2 * TD])
                - SHIFT * krylov[j, :, lanes(c)]
            )

    def pair_row(i, j):
        total = None
        for c in range(COMP):
            term = krylov[i, :, lanes(c)] * krylov[j, :, lanes(c)]
            total = term if total is None else total + term
        return jnp.sum(total, axis=0, keepdims=True)

    all_copies = list(ghost_copies)
    for j in range(ITERS):
        spread_vector(j)
        if j == 0:
            load_up.wait()
            load_down.wait()
        copies = send_couplings(j)
        all_copies.extend(copies)
        if j == 0:
            for s in range(SLOTS):
                ghost_copies[s].wait_recv()
                index = jnp.broadcast_to(ghosts[s], (TILE, TILE))
                sub = lax.broadcasted_iota(jnp.int32, (TILE, TILE), 0)
                chosen = jnp.where(jnp.bitwise_and(index, TILE - 1) == sub, 1.0, 0.0)
                pick[s * TILE : (s + 1) * TILE, :] = chosen.T.astype(BF16)
                row = jnp.broadcast_to(ghosts[s], (2 * TD, TILE))
                where = jnp.where(jnp.right_shift(row, 7) == sub16, 1.0, 0.0)
                if s >= W:
                    where = where * live[0, s - W].astype(F32)
                place[s] = where.astype(BF16)
        own = multiply_own(j)
        finish(j, own, copies)

    sub = lax.broadcasted_iota(jnp.int32, (2 * TD, TILE), 0)
    lane = lax.broadcasted_iota(jnp.int32, (2 * TD, TILE), 1)
    total = jnp.zeros((2 * TD, TILE), F32)
    for position, (i, j) in enumerate(PAIRS):
        total = jnp.where(sub == position, pair_row(i, j), total)
    total = jnp.where(lane == sub, jnp.sum(total, axis=1, keepdims=True), 0.0)
    mine = jnp.sum(total, axis=0, keepdims=True)
    part_a[...] = mine
    other = pltpu.make_async_remote_copy(
        src_ref=part_a,
        dst_ref=recv_a,
        send_sem=send_a,
        recv_sem=got_a,
        device_id=(partner,),
        device_id_type=MESH,
    )
    other.start()
    other.wait_recv()
    last = len(OFFSETS)
    recv_b[last : last + 1, :] = mine + recv_a[...]
    for d in range(last):
        pltpu.make_async_remote_copy(
            src_ref=recv_b.at[pl.ds(last, 1)],
            dst_ref=recv_b.at[pl.ds(d, 1)],
            send_sem=send_b,
            recv_sem=got_b,
            device_id=(chips[d],),
            device_id_type=MESH,
        ).start()
    for j in range(1, ITERS):
        for t in range(TD):
            for c in range(COMP):
                nodes[j - 1, c : c + 1, lanes(t)] = krylov[j, t : t + 1, lanes(c)]
    arrived = recv_b.at[pl.ds(0, last)]
    pltpu.make_async_copy(arrived, arrived, got_b).wait()
    sums = jnp.sum(recv_b[...], axis=0, keepdims=True)
    gram = {
        pair: jnp.broadcast_to(sums[:, position : position + 1], (TD, TILE))
        for position, pair in enumerate(PAIRS)
    }
    weights = [weight[:COMP] for weight in small_solve(gram)]
    for t in range(TD):
        value = weights[0] * rhs[:, lanes(t)]
        for j in range(1, ITERS):
            value = value + weights[j] * nodes[j - 1, :, lanes(t)]
        out_ref[:, lanes(t)] = value
    for copy in all_copies + [other]:
        copy.wait_send()
    pltpu.make_async_copy(arrived, arrived, send_b).wait()


def local(n, *arrays):
    anywhere = pl.BlockSpec(memory_space=pl.ANY)
    smem = pltpu.SMEM
    vmem = pltpu.VMEM
    dma = pltpu.SemaphoreType.DMA
    rhs = arrays[0]
    return pl.pallas_call(
        functools.partial(kernel, n),
        out_shape=jax.ShapeDtypeStruct(rhs.shape, F32),
        in_specs=[anywhere] * 9,
        out_specs=pl.BlockSpec(memory_space=pltpu.VMEM),
        scratch_shapes=[
            smem((KL, TD), jnp.int32),
            smem((1, SLOTS), jnp.int32),
            smem((1, W), jnp.int32),
            vmem((SLOTS + PER_ROW * TD, WIDTH, WIDTH), BF16),
            vmem(rhs.shape, F32),
            vmem((ITERS + 1, TD, WIDTH), F32),
            vmem((ITERS - 1,) + rhs.shape, F32),
            vmem((TD, 2 * TD, WIDTH), BF16),
            vmem((TD * KL, 2 * TD, TILE), BF16),
            vmem((SLOTS, 1, TILE), jnp.int32),
            vmem((SLOTS * TILE, TILE), BF16),
            vmem((SLOTS, 2 * TD, TILE), BF16),
            vmem((ITERS, SLOTS, TD, TILE), F32),
            vmem((ITERS, SLOTS, TD, TILE), F32),
            vmem((1, TILE), F32),
            vmem((1, TILE), F32),
            vmem((len(OFFSETS) + 1, TILE), F32),
            dma((6 + 2 * TD,)),
            dma((SLOTS,)),
            dma((SLOTS,)),
            dma((ITERS, SLOTS)),
            dma((ITERS, SLOTS)),
            dma,
            dma,
            dma,
            dma,
        ],
        compiler_params=pltpu.CompilerParams(
            collective_id=0, has_side_effects=True, vmem_limit_bytes=65_000_000
        ),
    )(*arrays[:5], arrays[5].T, arrays[6], jnp.swapaxes(arrays[7], 0, 1), arrays[8])


def solution(mesh):
    in_specs = (
        P(None, "parts"),
        P("parts", None, None),
        P("parts", None, None, None),
        P("parts", None, None),
        P("parts", None, None),
        P("parts", None),
        P("parts", None),
        P("parts", None, None),
        P("parts", None),
    )
    return jax.shard_map(
        functools.partial(local, mesh.shape["parts"]),
        mesh=mesh,
        in_specs=in_specs,
        out_specs=P(None, "parts"),
        check_vma=False,
    )
```

```python
import functools
import itertools

import jax
import jax.numpy as jnp
from jax import lax
from jax.experimental import pallas as pl
from jax.experimental.pallas import tpu as pltpu
from jax.sharding import PartitionSpec as P

COMP = 4
TILE = 128
TD = 8
KL = 3
W = 3
ITERS = 3
WIDTH = COMP * TILE
SLOTS = 2 * W
PER_ROW = KL + 1
SHIFT = 2.0
EPS = 1e-06
MESH = pl.DeviceIdType.MESH
F32 = jnp.float32
BF16 = jnp.bfloat16
SIDE = 4
OFFSETS = sorted(
    itertools.product(range(SIDE), repeat=3), key=lambda d: -sum(min(k, SIDE - k) for k in d)
)[:-1]
LATE = {(i, ITERS): i for i in range(ITERS + 1)}
EARLY = {
    pair: TD + position
    for position, pair in enumerate((i, j) for i in range(ITERS) for j in range(i, ITERS))
}


def lanes(c):
    return slice(c * TILE, (c + 1) * TILE)


def halves(x):
    high = x.astype(BF16).astype(F32)
    return jnp.concatenate([high, x - high], axis=0).astype(BF16)


def small_solve(gram):
    n = ITERS + 1

    def g(i, j):
        return gram[(min(i, j), max(i, j))]

    def dot(u, v):
        total = None
        for i, a in u.items():
            for j, b in v.items():
                term = a * b * g(i, j)
                total = term if total is None else total + term
        return total

    beta = jnp.sqrt(g(0, 0) + EPS)
    basis = [{0: 1.0 / beta}]
    hess = {}
    for j in range(ITERS):
        w = {}
        for i, a in basis[j].items():
            w[i + 1] = a + w[i + 1] if i + 1 in w else a
            w[i] = SHIFT * a + w[i] if i in w else SHIFT * a
        for i in range(j + 1):
            hess[i, j] = dot(w, basis[i])
            for k, b in basis[i].items():
                w[k] = w[k] - hess[i, j] * b
        scale = jnp.sqrt(jnp.maximum(dot(w, w), 0.0) + EPS)
        hess[j + 1, j] = scale
        if j + 1 < ITERS:
            inverse = 1.0 / scale
            basis.append({k: a * inverse for k, a in w.items()})
    normal = {}
    for a in range(ITERS):
        for b in range(a + 1):
            normal[a, b] = sum(
                hess[i, a] * hess[i, b] for i in range(n) if (i, a) in hess and (i, b) in hess
            )
    target = [beta * hess[0, j] for j in range(ITERS)]
    low = {}
    inv = []
    for a in range(ITERS):
        for b in range(a):
            value = normal[a, b]
            for k in range(b):
                value = value - low[a, k] * low[b, k]
            low[a, b] = value * inv[b]
        value = normal[a, a]
        for k in range(a):
            value = value - low[a, k] * low[a, k]
        inv.append(1.0 / jnp.sqrt(value))
    inner = []
    for a in range(ITERS):
        value = target[a]
        for k in range(a):
            value = value - low[a, k] * inner[k]
        inner.append(value * inv[a])
    weights = [None] * ITERS
    for a in reversed(range(ITERS)):
        value = inner[a]
        for k in range(a + 1, ITERS):
            value = value - low[k, a] * weights[k]
        weights[a] = value * inv[a]
    out = []
    for i in range(ITERS):
        out.append(sum(weights[j] * basis[j][i] for j in range(ITERS) if i in basis[j]))
    return out


def kernel(
    n,
    rhs_hbm,
    diag_hbm,
    local_hbm,
    up_hbm,
    down_hbm,
    pattern_hbm,
    rows_hbm,
    ghost_hbm,
    live_hbm,
    out_ref,
    pattern,
    rows,
    live,
    tiles,
    rhs,
    krylov,
    nodes,
    spread,
    masks,
    ghosts,
    pick,
    place,
    sent,
    got,
    part_a,
    recv_a,
    recv_b,
    load_sem,
    ghost_send,
    ghost_recv,
    halo_send,
    halo_recv,
    send_a,
    got_a,
    send_b,
    got_b,
):
    me = lax.axis_index("parts")
    around = [lax.rem(me + s + 1, n) for s in range(W)] + [
        lax.rem(me + n - s - 1, n) for s in range(W)
    ]
    barrier = pltpu.get_barrier_semaphore()
    for other in around:
        pl.semaphore_signal(barrier, inc=1, device_id=(other,), device_id_type=MESH)
    core = lax.rem(me, 2)
    digits = [lax.rem(me // 2, SIDE), lax.rem(me // (2 * SIDE), SIDE), me // (2 * SIDE * SIDE)]
    moved = [
        [2 * SIDE**axis * lax.rem(digits[axis] + d, SIDE) for d in range(SIDE)] for axis in range(3)
    ]
    partner = me + 1 - 2 * core
    chips = [core + moved[0][dx] + moved[1][dz] + moved[2][dy] for dx, dz, dy in OFFSETS]

    loads = []

    def load(source, target):
        copy = pltpu.make_async_copy(source, target, load_sem.at[len(loads)])
        copy.start()
        loads.append(copy)
        return copy

    load_rhs = load(rhs_hbm, rhs)
    load_small = [load(rows_hbm, rows), load(live_hbm, live), load(pattern_hbm, pattern)]
    load_up = load(up_hbm, tiles.at[pl.ds(0, W)])
    load_down = load(down_hbm, tiles.at[pl.ds(W, W)])
    load_rows = []
    for t in range(TD):
        first = SLOTS + PER_ROW * t
        load_rows.append(
            (
                load(diag_hbm.at[t], tiles.at[first]),
                load(local_hbm.at[t], tiles.at[pl.ds(first + 1, KL)]),
            )
        )

    for other in [partner] + chips:
        pl.semaphore_signal(barrier, inc=1, device_id=(other,), device_id_type=MESH)
    for copy in load_small:
        copy.wait()
    sub16 = lax.rem(lax.broadcasted_iota(jnp.int32, (2 * TD, TILE), 0), TD)
    sub8 = lax.broadcasted_iota(jnp.int32, (TD, TILE), 0)
    for t in range(TD):
        for k in range(KL):
            masks[KL * t + k] = jnp.where(sub16 == pattern[k, t], 1.0, 0.0).astype(BF16)

    load_rhs.wait()
    for t in range(TD):
        for c in range(COMP):
            krylov[0, t : t + 1, lanes(c)] = rhs[c : c + 1, lanes(t)]

    def spread_vector(j):
        for t in range(TD):
            row = jnp.broadcast_to(krylov[j, t : t + 1, :], (TD, WIDTH))
            spread[t] = halves(row)

    far = 1 - lax.rem(me, 2 * SIDE) // SIDE
    orders = []
    for side in range(2):
        down = far if side == 0 else 1 - far
        for k in range(W):
            target = lax.rem(me + n + (k + 1) * (1 - 2 * down), n)
            orders.append((W * down + k, k, down, target))

    def couple(j, chosen):
        found = []
        for s, k, down, target in chosen:
            left = spread[rows[0, s]]
            found.append(jnp.dot(left, tiles[s], preferred_element_type=F32))
        for (s, k, down, target), both in zip(chosen, found):
            term = both[:TD] + both[TD:]
            message = term[:, lanes(0)]
            for c in range(1, COMP):
                message = jnp.where(sub8 == c, term[:, lanes(c)], message)
            factor = (down + (1 - down) * live[0, k]).astype(F32)
            sent[j, s] = (message * factor)[:COMP]

    def send(j, chosen):
        copies = []
        for s, k, down, target in chosen:
            copy = pltpu.make_async_remote_copy(
                src_ref=sent.at[j, s],
                dst_ref=got.at[j, s],
                send_sem=halo_send.at[j, s],
                recv_sem=halo_recv.at[j, s],
                device_id=(target,),
                device_id_type=MESH,
            )
            copy.start()
            copies.append(copy)
        return copies

    def wait_halo(j):
        for s in range(SLOTS):
            pltpu.make_async_copy(got.at[j, s], got.at[j, s], halo_recv.at[j, s]).wait()

    def multiply_own(j):
        total = None
        for t in range(TD):
            if j == 0:
                for copy in load_rows[t]:
                    copy.wait()
            vector = spread[t]
            for k in range(PER_ROW):
                if k == 0:
                    mask = jnp.where(sub16 == t, 1.0, 0.0).astype(BF16)
                else:
                    mask = masks[KL * t + k - 1]
                left = vector * jnp.concatenate([mask] * COMP, axis=1)
                part = jnp.dot(left, tiles[SLOTS + PER_ROW * t + k], preferred_element_type=F32)
                total = part if total is None else total + part
        return total[:TD] + total[TD:]

    def finish(j, own):
        wait_halo(j)
        left = []
        for c in range(COMP):
            blocks = []
            for s in range(SLOTS):
                row = jnp.broadcast_to(got[j, s, c : c + 1, :], (TD, TILE))
                blocks.append(halves(row) * place[s])
            left.append(jnp.concatenate(blocks, axis=1))
        added = jnp.dot(jnp.concatenate(left, axis=0), pick[...], preferred_element_type=F32)
        for c in range(COMP):
            first = 2 * TD * c
            krylov[j + 1, :, lanes(c)] = (
                own[:, lanes(c)]
                + (added[first : first + TD] + added[first + TD : first + 2 * TD])
                - SHIFT * krylov[j, :, lanes(c)]
            )

    def pair_row(i, j):
        total = None
        for c in range(COMP):
            term = krylov[i, :, lanes(c)] * krylov[j, :, lanes(c)]
            total = term if total is None else total + term
        return jnp.sum(total, axis=0, keepdims=True)

    lane8 = lax.broadcasted_iota(jnp.int32, (TD, TILE), 1)

    def gather_pairs(pairs):
        total = jnp.zeros((TD, TILE), F32)
        first = min(pairs.values())
        for (i, j), position in pairs.items():
            total = jnp.where(sub8 == position - first, pair_row(i, j), total)
        total = jnp.where(lane8 == sub8 + first, jnp.sum(total, axis=1, keepdims=True), 0.0)
        return jnp.sum(total, axis=0, keepdims=True)

    all_copies = []
    for j in range(ITERS):
        spread_vector(j)
        if j == 0:
            load_up.wait()
            load_down.wait()
            couple(j, orders)
            pl.semaphore_wait(barrier, SLOTS + 1 + len(chips))
            ghost_copies = []
            for s in range(SLOTS):
                copy = pltpu.make_async_remote_copy(
                    src_ref=ghost_hbm.at[s],
                    dst_ref=ghosts.at[s],
                    send_sem=ghost_send.at[s],
                    recv_sem=ghost_recv.at[s],
                    device_id=(around[s],),
                    device_id_type=MESH,
                )
                copy.start()
                ghost_copies.append(copy)
            all_copies.extend(ghost_copies)
            all_copies.extend(send(j, orders))
        else:
            for chosen in (orders[:W], orders[W:]):
                couple(j, chosen)
                all_copies.extend(send(j, chosen))
        own = multiply_own(j)
        if j == 0:
            sub = lax.broadcasted_iota(jnp.int32, (TILE, TILE), 0)
            for s in range(SLOTS):
                ghost_copies[s].wait_recv()
                index = jnp.broadcast_to(ghosts[s], (TILE, TILE))
                chosen = jnp.where(jnp.bitwise_and(index, TILE - 1) == sub, 1.0, 0.0)
                pick[s * TILE : (s + 1) * TILE, :] = chosen.T.astype(BF16)
                row = jnp.broadcast_to(ghosts[s], (2 * TD, TILE))
                where = jnp.where(jnp.right_shift(row, 7) == sub16, 1.0, 0.0)
                if s >= W:
                    where = where * live[0, s - W].astype(F32)
                place[s] = where.astype(BF16)
        if j + 1 == ITERS:
            early = gather_pairs(EARLY)
        finish(j, own)
    mine = early + gather_pairs(LATE)
    part_a[...] = mine
    other = pltpu.make_async_remote_copy(
        src_ref=part_a,
        dst_ref=recv_a,
        send_sem=send_a,
        recv_sem=got_a,
        device_id=(partner,),
        device_id_type=MESH,
    )
    other.start()
    other.wait_recv()
    last = len(OFFSETS)
    recv_b[last : last + 1, :] = mine + recv_a[...]
    for d in range(last):
        pltpu.make_async_remote_copy(
            src_ref=recv_b.at[pl.ds(last, 1)],
            dst_ref=recv_b.at[pl.ds(d, 1)],
            send_sem=send_b,
            recv_sem=got_b,
            device_id=(chips[d],),
            device_id_type=MESH,
        ).start()
    for j in range(1, ITERS):
        for t in range(TD):
            for c in range(COMP):
                nodes[j - 1, c : c + 1, lanes(t)] = krylov[j, t : t + 1, lanes(c)]
    arrived = recv_b.at[pl.ds(0, last)]
    pltpu.make_async_copy(arrived, arrived, got_b).wait()
    sums = jnp.sum(recv_b[...], axis=0, keepdims=True)
    gram = {
        pair: jnp.broadcast_to(sums[:, position : position + 1], (TD, TILE))
        for pair, position in (EARLY | LATE).items()
    }
    weights = [weight[:COMP] for weight in small_solve(gram)]
    for t in range(TD):
        value = weights[0] * rhs[:, lanes(t)]
        for j in range(1, ITERS):
            value = value + weights[j] * nodes[j - 1, :, lanes(t)]
        out_ref[:, lanes(t)] = value
    for copy in all_copies + [other]:
        copy.wait_send()
    pltpu.make_async_copy(arrived, arrived, send_b).wait()


def local(n, *arrays):
    anywhere = pl.BlockSpec(memory_space=pl.ANY)
    smem = pltpu.SMEM
    vmem = pltpu.VMEM
    dma = pltpu.SemaphoreType.DMA
    rhs = arrays[0]
    return pl.pallas_call(
        functools.partial(kernel, n),
        out_shape=pltpu.VMEM(rhs.shape, F32),
        in_specs=[anywhere] * 9,
        out_specs=pl.BlockSpec(memory_space=pltpu.VMEM),
        scratch_shapes=[
            smem((KL, TD), jnp.int32),
            smem((1, SLOTS), jnp.int32),
            smem((1, W), jnp.int32),
            vmem((SLOTS + PER_ROW * TD, WIDTH, WIDTH), BF16),
            vmem(rhs.shape, F32),
            vmem((ITERS + 1, TD, WIDTH), F32),
            vmem((ITERS - 1,) + rhs.shape, F32),
            vmem((TD, 2 * TD, WIDTH), BF16),
            vmem((TD * KL, 2 * TD, TILE), BF16),
            vmem((SLOTS, 1, TILE), jnp.int32),
            vmem((SLOTS * TILE, TILE), BF16),
            vmem((SLOTS, 2 * TD, TILE), BF16),
            vmem((ITERS, SLOTS, COMP, TILE), F32),
            vmem((ITERS, SLOTS, COMP, TILE), F32),
            vmem((1, TILE), F32),
            vmem((1, TILE), F32),
            vmem((len(OFFSETS) + 1, TILE), F32),
            dma((6 + 2 * TD,)),
            dma((SLOTS,)),
            dma((SLOTS,)),
            dma((ITERS, SLOTS)),
            dma((ITERS, SLOTS)),
            dma,
            dma,
            dma,
            dma,
        ],
        compiler_params=pltpu.CompilerParams(
            collective_id=0, has_side_effects=True, vmem_limit_bytes=65_000_000
        ),
    )(*arrays[:5], arrays[5].T, arrays[6], jnp.swapaxes(arrays[7], 0, 1), arrays[8])


def solution(mesh):
    in_specs = (
        P(None, "parts"),
        P("parts", None, None),
        P("parts", None, None, None),
        P("parts", None, None),
        P("parts", None, None),
        P("parts", None),
        P("parts", None),
        P("parts", None, None),
        P("parts", None),
    )
    return jax.shard_map(
        functools.partial(local, mesh.shape["parts"]),
        mesh=mesh,
        in_specs=in_specs,
        out_specs=P(None, "parts"),
        check_vma=False,
    )
```

```python
import functools

import jax
import jax.numpy as jnp
from jax import lax
from jax.experimental import pallas as pl
from jax.experimental.pallas import tpu as pltpu
from jax.sharding import PartitionSpec as P

COMP = 4
TILE = 128
TD = 8
KL = 3
W = 3
ITERS = 3
WIDTH = COMP * TILE
SLOTS = 2 * W
PER_ROW = KL + 1
SHIFT = 2.0
EPS = 1e-06
MESH = pl.DeviceIdType.MESH
F32 = jnp.float32
BF16 = jnp.bfloat16
SIDE = 4
LATE = {(i, ITERS): i for i in range(ITERS + 1)}
EARLY = {
    pair: TD + position
    for position, pair in enumerate((i, j) for i in range(ITERS) for j in range(i, ITERS))
}


def lanes(c):
    return slice(c * TILE, (c + 1) * TILE)


def halves(x):
    high = x.astype(BF16).astype(F32)
    return jnp.concatenate([high, x - high], axis=0).astype(BF16)


def small_solve(gram):
    n = ITERS + 1

    def g(i, j):
        return gram[(min(i, j), max(i, j))]

    def dot(u, v):
        total = None
        for i, a in u.items():
            for j, b in v.items():
                term = a * b * g(i, j)
                total = term if total is None else total + term
        return total

    beta = jnp.sqrt(g(0, 0) + EPS)
    basis = [{0: 1.0 / beta}]
    hess = {}
    for j in range(ITERS):
        w = {}
        for i, a in basis[j].items():
            w[i + 1] = a + w[i + 1] if i + 1 in w else a
            w[i] = SHIFT * a + w[i] if i in w else SHIFT * a
        for i in range(j + 1):
            hess[i, j] = dot(w, basis[i])
            for k, b in basis[i].items():
                w[k] = w[k] - hess[i, j] * b
        scale = jnp.sqrt(jnp.maximum(dot(w, w), 0.0) + EPS)
        hess[j + 1, j] = scale
        if j + 1 < ITERS:
            inverse = 1.0 / scale
            basis.append({k: a * inverse for k, a in w.items()})
    normal = {}
    for a in range(ITERS):
        for b in range(a + 1):
            normal[a, b] = sum(
                hess[i, a] * hess[i, b] for i in range(n) if (i, a) in hess and (i, b) in hess
            )
    target = [beta * hess[0, j] for j in range(ITERS)]
    low = {}
    inv = []
    for a in range(ITERS):
        for b in range(a):
            value = normal[a, b]
            for k in range(b):
                value = value - low[a, k] * low[b, k]
            low[a, b] = value * inv[b]
        value = normal[a, a]
        for k in range(a):
            value = value - low[a, k] * low[a, k]
        inv.append(1.0 / jnp.sqrt(value))
    inner = []
    for a in range(ITERS):
        value = target[a]
        for k in range(a):
            value = value - low[a, k] * inner[k]
        inner.append(value * inv[a])
    weights = [None] * ITERS
    for a in reversed(range(ITERS)):
        value = inner[a]
        for k in range(a + 1, ITERS):
            value = value - low[k, a] * weights[k]
        weights[a] = value * inv[a]
    out = []
    for i in range(ITERS):
        out.append(sum(weights[j] * basis[j][i] for j in range(ITERS) if i in basis[j]))
    return out


def kernel(
    n,
    rhs_hbm,
    diag_hbm,
    local_hbm,
    up_hbm,
    down_hbm,
    pattern_hbm,
    rows_hbm,
    ghost_hbm,
    live_hbm,
    out_ref,
    pattern,
    rows,
    live,
    tiles,
    rhs,
    krylov,
    nodes,
    spread,
    masks,
    ghosts,
    pick,
    place,
    sent,
    got,
    recv,
    load_sem,
    ghost_send,
    ghost_recv,
    halo_send,
    halo_recv,
    present,
    all_send,
    all_got,
):
    me = lax.axis_index("parts")
    around = [lax.rem(me + s + 1, n) for s in range(W)] + [
        lax.rem(me + n - s - 1, n) for s in range(W)
    ]
    core = lax.rem(me, 2)
    digits = [lax.rem(me // 2, SIDE), lax.rem(me // (2 * SIDE), SIDE), me // (2 * SIDE * SIDE)]
    moved = [
        [2 * SIDE**axis * lax.rem(digits[axis] + d, SIDE) for d in range(SIDE)] for axis in range(3)
    ]
    lines = [
        [me - moved[axis][0] + moved[axis][d] for d in range(1, SIDE)] for axis in range(3)
    ]
    greeted = around + lines[0] + lines[1] + lines[2]
    barrier = pltpu.get_barrier_semaphore()
    for other in greeted:
        pl.semaphore_signal(barrier, inc=1, device_id=(other,), device_id_type=MESH)
    partner = me + 1 - 2 * core

    loads = []

    def load(source, target):
        copy = pltpu.make_async_copy(source, target, load_sem.at[len(loads)])
        copy.start()
        loads.append(copy)
        return copy

    load_rhs = load(rhs_hbm, rhs)
    load_small = [load(rows_hbm, rows), load(live_hbm, live), load(pattern_hbm, pattern)]
    load_up = load(up_hbm, tiles.at[pl.ds(0, W)])
    load_down = load(down_hbm, tiles.at[pl.ds(W, W)])
    load_rows = []
    for t in range(TD):
        first = SLOTS + PER_ROW * t
        load_rows.append(
            (
                load(diag_hbm.at[t], tiles.at[first]),
                load(local_hbm.at[t], tiles.at[pl.ds(first + 1, KL)]),
            )
        )

    for copy in load_small:
        copy.wait()
    sub16 = lax.rem(lax.broadcasted_iota(jnp.int32, (2 * TD, TILE), 0), TD)
    sub8 = lax.broadcasted_iota(jnp.int32, (TD, TILE), 0)
    for t in range(TD):
        for k in range(KL):
            masks[KL * t + k] = jnp.where(sub16 == pattern[k, t], 1.0, 0.0).astype(BF16)

    load_rhs.wait()
    for t in range(TD):
        for c in range(COMP):
            krylov[0, t : t + 1, lanes(c)] = rhs[c : c + 1, lanes(t)]

    def spread_vector(j):
        for t in range(TD):
            row = jnp.broadcast_to(krylov[j, t : t + 1, :], (TD, WIDTH))
            spread[t] = halves(row)

    far = 1 - lax.rem(me, 2 * SIDE) // SIDE
    orders = []
    for side in range(2):
        down = far if side == 0 else 1 - far
        for k in range(W):
            target = lax.rem(me + n + (k + 1) * (1 - 2 * down), n)
            orders.append((W * down + k, k, down, target))

    def couple(j, chosen):
        found = []
        for s, k, down, target in chosen:
            left = spread[rows[0, s]]
            found.append(jnp.dot(left, tiles[s], preferred_element_type=F32))
        for (s, k, down, target), both in zip(chosen, found):
            term = both[:TD] + both[TD:]
            message = term[:, lanes(0)]
            for c in range(1, COMP):
                message = jnp.where(sub8 == c, term[:, lanes(c)], message)
            factor = (down + (1 - down) * live[0, k]).astype(F32)
            sent[j, s] = (message * factor)[:COMP]

    def send(j, chosen):
        copies = []
        for s, k, down, target in chosen:
            copy = pltpu.make_async_remote_copy(
                src_ref=sent.at[j, s],
                dst_ref=got.at[j, s],
                send_sem=halo_send.at[j, s],
                recv_sem=halo_recv.at[j, s],
                device_id=(target,),
                device_id_type=MESH,
            )
            copy.start()
            copies.append(copy)
        return copies

    def wait_halo(j):
        for s in range(SLOTS):
            pltpu.make_async_copy(got.at[j, s], got.at[j, s], halo_recv.at[j, s]).wait()

    def multiply_own(j):
        total = None
        for t in range(TD):
            if j == 0:
                for copy in load_rows[t]:
                    copy.wait()
            vector = spread[t]
            for k in range(PER_ROW):
                if k == 0:
                    mask = jnp.where(sub16 == t, 1.0, 0.0).astype(BF16)
                else:
                    mask = masks[KL * t + k - 1]
                left = vector * jnp.concatenate([mask] * COMP, axis=1)
                part = jnp.dot(left, tiles[SLOTS + PER_ROW * t + k], preferred_element_type=F32)
                total = part if total is None else total + part
        return total[:TD] + total[TD:]

    def finish(j, own):
        wait_halo(j)
        left = []
        for c in range(COMP):
            blocks = []
            for s in range(SLOTS):
                row = jnp.broadcast_to(got[j, s, c : c + 1, :], (TD, TILE))
                blocks.append(halves(row) * place[s])
            left.append(jnp.concatenate(blocks, axis=1))
        added = jnp.dot(jnp.concatenate(left, axis=0), pick[...], preferred_element_type=F32)
        for c in range(COMP):
            first = 2 * TD * c
            krylov[j + 1, :, lanes(c)] = (
                own[:, lanes(c)]
                + (added[first : first + TD] + added[first + TD : first + 2 * TD])
                - SHIFT * krylov[j, :, lanes(c)]
            )

    def pair_row(i, j):
        total = None
        for c in range(COMP):
            term = krylov[i, :, lanes(c)] * krylov[j, :, lanes(c)]
            total = term if total is None else total + term
        return jnp.sum(total, axis=0, keepdims=True)

    lane8 = lax.broadcasted_iota(jnp.int32, (TD, TILE), 1)

    def gather_pairs(pairs):
        total = jnp.zeros((TD, TILE), F32)
        first = min(pairs.values())
        for (i, j), position in pairs.items():
            total = jnp.where(sub8 == position - first, pair_row(i, j), total)
        total = jnp.where(lane8 == sub8 + first, jnp.sum(total, axis=1, keepdims=True), 0.0)
        return jnp.sum(total, axis=0, keepdims=True)

    all_copies = []
    for j in range(ITERS):
        spread_vector(j)
        if j == 0:
            load_up.wait()
            load_down.wait()
            couple(j, orders)
            pl.semaphore_wait(barrier, len(greeted))
            for chosen in (orders[:W], orders[W:]):
                for s, k, down, target in chosen:
                    copy = pltpu.make_async_remote_copy(
                        src_ref=ghost_hbm.at[s],
                        dst_ref=ghosts.at[s],
                        send_sem=ghost_send.at[s],
                        recv_sem=ghost_recv.at[s],
                        device_id=(target,),
                        device_id_type=MESH,
                    )
                    copy.start()
                    all_copies.append(copy)
                all_copies.extend(send(j, chosen))
        else:
            for chosen in (orders[:W], orders[W:]):
                couple(j, chosen)
                all_copies.extend(send(j, chosen))
        others = [lines[1], lines[2], [partner]][j]
        for other in others:
            pl.semaphore_signal(
                present.at[j], inc=1, device_id=(other,), device_id_type=MESH
            )
        own = multiply_own(j)
        pl.semaphore_wait(present.at[j], len(others))
        if j == 0:
            sub = lax.broadcasted_iota(jnp.int32, (TILE, TILE), 0)
            for s, k, down, target in orders:
                pltpu.make_async_copy(ghosts.at[s], ghosts.at[s], ghost_recv.at[s]).wait()
                index = jnp.broadcast_to(ghosts[s], (TILE, TILE))
                hit = jnp.where(jnp.bitwise_and(index, TILE - 1) == sub, 1.0, 0.0)
                pick[pl.ds(pl.multiple_of(s * TILE, TILE), TILE), :] = hit.T.astype(BF16)
                row = jnp.broadcast_to(ghosts[s], (2 * TD, TILE))
                hit = jnp.where(jnp.right_shift(row, 7) == sub16, 1.0, 0.0)
                place[s] = (hit * (1 - down + down * live[0, k]).astype(F32)).astype(BF16)
        if j + 1 == ITERS:
            early = gather_pairs(EARLY)
        finish(j, own)
    mine = early + gather_pairs(LATE)
    recv[pl.ds(me, 1), :] = mine
    for d in range(n - 1):
        target = d + jnp.minimum(jnp.maximum(d + 1 - me, 0), 1)
        pltpu.make_async_remote_copy(
            src_ref=recv.at[pl.ds(me, 1)],
            dst_ref=recv.at[pl.ds(me, 1)],
            send_sem=all_send,
            recv_sem=all_got,
            device_id=(target,),
            device_id_type=MESH,
        ).start()
    for j in range(1, ITERS):
        for t in range(TD):
            for c in range(COMP):
                nodes[j - 1, c : c + 1, lanes(t)] = krylov[j, t : t + 1, lanes(c)]
    arrived = recv.at[pl.ds(0, n - 1)]
    pltpu.make_async_copy(arrived, arrived, all_got).wait()
    sums = jnp.sum(recv[...], axis=0, keepdims=True)
    gram = {
        pair: jnp.broadcast_to(sums[:, position : position + 1], (TD, TILE))
        for pair, position in (EARLY | LATE).items()
    }
    weights = [weight[:COMP] for weight in small_solve(gram)]
    for t in range(TD):
        value = weights[0] * rhs[:, lanes(t)]
        for j in range(1, ITERS):
            value = value + weights[j] * nodes[j - 1, :, lanes(t)]
        out_ref[:, lanes(t)] = value
    for copy in all_copies:
        copy.wait_send()
    pltpu.make_async_copy(arrived, arrived, all_send).wait()


def local(n, *arrays):
    anywhere = pl.BlockSpec(memory_space=pl.ANY)
    smem = pltpu.SMEM
    vmem = pltpu.VMEM
    dma = pltpu.SemaphoreType.DMA
    rhs = arrays[0]
    return pl.pallas_call(
        functools.partial(kernel, n),
        out_shape=pltpu.VMEM(rhs.shape, F32),
        in_specs=[anywhere] * 9,
        out_specs=pl.BlockSpec(memory_space=pltpu.VMEM),
        scratch_shapes=[
            smem((KL, TD), jnp.int32),
            smem((1, SLOTS), jnp.int32),
            smem((1, W), jnp.int32),
            vmem((SLOTS + PER_ROW * TD, WIDTH, WIDTH), BF16),
            vmem(rhs.shape, F32),
            vmem((ITERS + 1, TD, WIDTH), F32),
            vmem((ITERS - 1,) + rhs.shape, F32),
            vmem((TD, 2 * TD, WIDTH), BF16),
            vmem((TD * KL, 2 * TD, TILE), BF16),
            vmem((SLOTS, 1, TILE), jnp.int32),
            vmem((SLOTS * TILE, TILE), BF16),
            vmem((SLOTS, 2 * TD, TILE), BF16),
            vmem((ITERS, SLOTS, COMP, TILE), F32),
            vmem((ITERS, SLOTS, COMP, TILE), F32),
            vmem((n, TILE), F32),
            dma((6 + 2 * TD,)),
            dma((SLOTS,)),
            dma((SLOTS,)),
            dma((ITERS, SLOTS)),
            dma((ITERS, SLOTS)),
            pltpu.SemaphoreType.REGULAR((ITERS,)),
            dma,
            dma,
        ],
        compiler_params=pltpu.CompilerParams(
            collective_id=0, has_side_effects=True, vmem_limit_bytes=65_000_000
        ),
    )(*arrays[:5], arrays[5].T, arrays[6], jnp.swapaxes(arrays[7], 0, 1), arrays[8])


def solution(mesh):
    in_specs = (
        P(None, "parts"),
        P("parts", None, None),
        P("parts", None, None, None),
        P("parts", None, None),
        P("parts", None, None),
        P("parts", None),
        P("parts", None),
        P("parts", None, None),
        P("parts", None),
    )
    return jax.shard_map(
        functools.partial(local, mesh.shape["parts"]),
        mesh=mesh,
        in_specs=in_specs,
        out_specs=P(None, "parts"),
        check_vma=False,
    )
```

```python
import functools

import jax
import jax.numpy as jnp
from jax import lax
from jax.experimental import pallas as pl
from jax.experimental.pallas import tpu as pltpu
from jax.sharding import PartitionSpec as P

COMP = 4
TILE = 128
TD = 8
KL = 3
W = 3
ITERS = 3
WIDTH = COMP * TILE
SLOTS = 2 * W
PER_ROW = KL + 1
SHIFT = 2.0
EPS = 1e-06
LAG = 2
MESH = pl.DeviceIdType.MESH
F32 = jnp.float32
BF16 = jnp.bfloat16
SIDE = 4
LATE = {(i, ITERS): i for i in range(ITERS + 1)}
EARLY = {
    pair: TD + position
    for position, pair in enumerate((i, j) for i in range(ITERS) for j in range(i, ITERS))
}


def lanes(c):
    return slice(c * TILE, (c + 1) * TILE)


def halves(x):
    high = x.astype(BF16).astype(F32)
    return jnp.concatenate([high, x - high], axis=0).astype(BF16)


def small_solve(gram):
    n = ITERS + 1

    def g(i, j):
        return gram[(min(i, j), max(i, j))]

    def dot(u, v):
        total = None
        for i, a in u.items():
            for j, b in v.items():
                term = a * b * g(i, j)
                total = term if total is None else total + term
        return total

    beta = jnp.sqrt(g(0, 0) + EPS)
    basis = [{0: 1.0 / beta}]
    hess = {}
    for j in range(ITERS):
        w = {}
        for i, a in basis[j].items():
            w[i + 1] = a + w[i + 1] if i + 1 in w else a
            w[i] = SHIFT * a + w[i] if i in w else SHIFT * a
        for i in range(j + 1):
            hess[i, j] = dot(w, basis[i])
            for k, b in basis[i].items():
                w[k] = w[k] - hess[i, j] * b
        scale = jnp.sqrt(jnp.maximum(dot(w, w), 0.0) + EPS)
        hess[j + 1, j] = scale
        if j + 1 < ITERS:
            inverse = 1.0 / scale
            basis.append({k: a * inverse for k, a in w.items()})
    normal = {}
    for a in range(ITERS):
        for b in range(a + 1):
            normal[a, b] = sum(
                hess[i, a] * hess[i, b] for i in range(n) if (i, a) in hess and (i, b) in hess
            )
    target = [beta * hess[0, j] for j in range(ITERS)]
    low = {}
    inv = []
    for a in range(ITERS):
        for b in range(a):
            value = normal[a, b]
            for k in range(b):
                value = value - low[a, k] * low[b, k]
            low[a, b] = value * inv[b]
        value = normal[a, a]
        for k in range(a):
            value = value - low[a, k] * low[a, k]
        inv.append(1.0 / jnp.sqrt(value))
    inner = []
    for a in range(ITERS):
        value = target[a]
        for k in range(a):
            value = value - low[a, k] * inner[k]
        inner.append(value * inv[a])
    weights = [None] * ITERS
    for a in reversed(range(ITERS)):
        value = inner[a]
        for k in range(a + 1, ITERS):
            value = value - low[k, a] * weights[k]
        weights[a] = value * inv[a]
    out = []
    for i in range(ITERS):
        out.append(sum(weights[j] * basis[j][i] for j in range(ITERS) if i in basis[j]))
    return out


def kernel(
    n,
    rhs_hbm,
    diag_hbm,
    local_hbm,
    up_hbm,
    down_hbm,
    pattern_hbm,
    rows_hbm,
    ghost_hbm,
    live_hbm,
    out_ref,
    pattern,
    rows,
    live,
    tiles,
    rhs,
    krylov,
    nodes,
    spread,
    masks,
    ghosts,
    pick,
    place,
    sent,
    got,
    recv,
    load_sem,
    ghost_send,
    ghost_recv,
    halo_send,
    halo_recv,
    present,
    all_send,
    all_got,
):
    me = lax.axis_index("parts")
    around = [lax.rem(me + s + 1, n) for s in range(W)] + [
        lax.rem(me + n - s - 1, n) for s in range(W)
    ]
    core = lax.rem(me, 2)
    digits = [lax.rem(me // 2, SIDE), lax.rem(me // (2 * SIDE), SIDE), me // (2 * SIDE * SIDE)]
    moved = [
        [2 * SIDE**axis * lax.rem(digits[axis] + d, SIDE) for d in range(SIDE)] for axis in range(3)
    ]
    lines = [
        [me - moved[axis][0] + moved[axis][d] for d in range(1, SIDE)] for axis in range(3)
    ]
    greeted = around + lines[0] + lines[1] + lines[2]
    barrier = pltpu.get_barrier_semaphore()
    for other in greeted:
        pl.semaphore_signal(barrier, inc=1, device_id=(other,), device_id_type=MESH)
    partner = me + 1 - 2 * core

    loads = []

    def load(source, target):
        copy = pltpu.make_async_copy(source, target, load_sem.at[len(loads)])
        copy.start()
        loads.append(copy)
        return copy

    load_rhs = load(rhs_hbm, rhs)
    load_small = [load(rows_hbm, rows), load(live_hbm, live), load(pattern_hbm, pattern)]
    load_up = load(up_hbm, tiles.at[pl.ds(0, W)])
    load_down = load(down_hbm, tiles.at[pl.ds(W, W)])
    load_rows = []
    for t in range(TD):
        first = SLOTS + PER_ROW * t
        load_rows.append(
            (
                load(diag_hbm.at[t], tiles.at[first]),
                load(local_hbm.at[t], tiles.at[pl.ds(first + 1, KL)]),
            )
        )

    for copy in load_small:
        copy.wait()
    sub16 = lax.rem(lax.broadcasted_iota(jnp.int32, (2 * TD, TILE), 0), TD)
    sub8 = lax.broadcasted_iota(jnp.int32, (TD, TILE), 0)
    for t in range(TD):
        for k in range(KL):
            masks[KL * t + k] = jnp.where(sub16 == pattern[k, t], 1.0, 0.0).astype(BF16)

    load_rhs.wait()
    for t in range(TD):
        for c in range(COMP):
            krylov[0, t : t + 1, lanes(c)] = rhs[c : c + 1, lanes(t)]

    def spread_vector(j):
        for t in range(TD):
            row = jnp.broadcast_to(krylov[j, t : t + 1, :], (TD, WIDTH))
            spread[t] = halves(row)

    all_copies = []
    far = 1 - lax.rem(me, 2 * SIDE) // SIDE
    orders = []
    for side in range(2):
        down = far if side == 0 else 1 - far
        for k in reversed(range(W)):
            target = lax.rem(me + n + (k + 1) * (1 - 2 * down), n)
            orders.append((W * down + k, k, down, target))

    def product(order):
        s = order[0]
        return jnp.dot(spread[rows[0, s]], tiles[s], preferred_element_type=F32)

    def keep(j, order, both):
        s, k, down, target = order
        term = both[:TD] + both[TD:]
        message = term[:, lanes(0)]
        for c in range(1, COMP):
            message = jnp.where(sub8 == c, term[:, lanes(c)], message)
        factor = (down + (1 - down) * live[0, k]).astype(F32)
        sent[j, s] = (message * factor)[:COMP]

    def send(j, order):
        s, k, down, target = order
        copy = pltpu.make_async_remote_copy(
            src_ref=sent.at[j, s],
            dst_ref=got.at[j, s],
            send_sem=halo_send.at[j, s],
            recv_sem=halo_recv.at[j, s],
            device_id=(target,),
            device_id_type=MESH,
        )
        copy.start()
        all_copies.append(copy)

    def wait_halo(j):
        for s in range(SLOTS):
            pltpu.make_async_copy(got.at[j, s], got.at[j, s], halo_recv.at[j, s]).wait()

    def multiply_own(j):
        total = None
        for t in range(TD):
            if j == 0:
                for copy in load_rows[t]:
                    copy.wait()
            vector = spread[t]
            for k in range(PER_ROW):
                if k == 0:
                    mask = jnp.where(sub16 == t, 1.0, 0.0).astype(BF16)
                else:
                    mask = masks[KL * t + k - 1]
                left = vector * jnp.concatenate([mask] * COMP, axis=1)
                part = jnp.dot(left, tiles[SLOTS + PER_ROW * t + k], preferred_element_type=F32)
                total = part if total is None else total + part
        return total[:TD] + total[TD:]

    def finish(j, own):
        wait_halo(j)
        left = []
        for c in range(COMP):
            blocks = []
            for s in range(SLOTS):
                row = jnp.broadcast_to(got[j, s, c : c + 1, :], (TD, TILE))
                blocks.append(halves(row) * place[s])
            left.append(jnp.concatenate(blocks, axis=1))
        added = jnp.dot(jnp.concatenate(left, axis=0), pick[...], preferred_element_type=F32)
        for c in range(COMP):
            first = 2 * TD * c
            krylov[j + 1, :, lanes(c)] = (
                own[:, lanes(c)]
                + (added[first : first + TD] + added[first + TD : first + 2 * TD])
                - SHIFT * krylov[j, :, lanes(c)]
            )

    def pair_row(i, j):
        total = None
        for c in range(COMP):
            term = krylov[i, :, lanes(c)] * krylov[j, :, lanes(c)]
            total = term if total is None else total + term
        return jnp.sum(total, axis=0, keepdims=True)

    lane8 = lax.broadcasted_iota(jnp.int32, (TD, TILE), 1)

    def gather_pairs(pairs):
        total = jnp.zeros((TD, TILE), F32)
        first = min(pairs.values())
        for (i, j), position in pairs.items():
            total = jnp.where(sub8 == position - first, pair_row(i, j), total)
        total = jnp.where(lane8 == sub8 + first, jnp.sum(total, axis=1, keepdims=True), 0.0)
        return jnp.sum(total, axis=0, keepdims=True)

    for j in range(ITERS):
        spread_vector(j)
        if j == 0:
            load_up.wait()
            load_down.wait()
            found = [product(order) for order in orders]
            for order, both in zip(orders, found):
                keep(j, order, both)
            pl.semaphore_wait(barrier, len(greeted))
            for chosen in (orders[:W], orders[W:]):
                for s, k, down, target in chosen:
                    copy = pltpu.make_async_remote_copy(
                        src_ref=ghost_hbm.at[s],
                        dst_ref=ghosts.at[s],
                        send_sem=ghost_send.at[s],
                        recv_sem=ghost_recv.at[s],
                        device_id=(target,),
                        device_id_type=MESH,
                    )
                    copy.start()
                    all_copies.append(copy)
                for order in chosen:
                    send(j, order)
        else:
            found = []
            for position in range(SLOTS + LAG):
                if position < SLOTS:
                    found.append(product(orders[position]))
                if position >= LAG:
                    keep(j, orders[position - LAG], found[position - LAG])
                    send(j, orders[position - LAG])
        others = [lines[1], lines[2], [partner]][j]
        for other in others:
            pl.semaphore_signal(
                present.at[j], inc=1, device_id=(other,), device_id_type=MESH
            )
        own = multiply_own(j)
        pl.semaphore_wait(present.at[j], len(others))
        if j == 0:
            sub = lax.broadcasted_iota(jnp.int32, (TILE, TILE), 0)
            for s, k, down, target in orders:
                pltpu.make_async_copy(ghosts.at[s], ghosts.at[s], ghost_recv.at[s]).wait()
                index = jnp.broadcast_to(ghosts[s], (TILE, TILE))
                hit = jnp.where(jnp.bitwise_and(index, TILE - 1) == sub, 1.0, 0.0)
                pick[pl.ds(pl.multiple_of(s * TILE, TILE), TILE), :] = hit.T.astype(BF16)
                row = jnp.broadcast_to(ghosts[s], (2 * TD, TILE))
                hit = jnp.where(jnp.right_shift(row, 7) == sub16, 1.0, 0.0)
                place[s] = (hit * (1 - down + down * live[0, k]).astype(F32)).astype(BF16)
        if j + 1 == ITERS:
            early = gather_pairs(EARLY)
        finish(j, own)
    mine = early + gather_pairs(LATE)
    recv[pl.ds(me, 1), :] = mine
    for d in range(n - 1):
        target = d + jnp.minimum(jnp.maximum(d + 1 - me, 0), 1)
        pltpu.make_async_remote_copy(
            src_ref=recv.at[pl.ds(me, 1)],
            dst_ref=recv.at[pl.ds(me, 1)],
            send_sem=all_send,
            recv_sem=all_got,
            device_id=(target,),
            device_id_type=MESH,
        ).start()
    for j in range(1, ITERS):
        for t in range(TD):
            for c in range(COMP):
                nodes[j - 1, c : c + 1, lanes(t)] = krylov[j, t : t + 1, lanes(c)]
    arrived = recv.at[pl.ds(0, n - 1)]
    pltpu.make_async_copy(arrived, arrived, all_got).wait()
    sums = jnp.sum(recv[...], axis=0, keepdims=True)
    gram = {
        pair: jnp.broadcast_to(sums[:, position : position + 1], (TD, TILE))
        for pair, position in (EARLY | LATE).items()
    }
    weights = [weight[:COMP] for weight in small_solve(gram)]
    for t in range(TD):
        value = weights[0] * rhs[:, lanes(t)]
        for j in range(1, ITERS):
            value = value + weights[j] * nodes[j - 1, :, lanes(t)]
        out_ref[:, lanes(t)] = value
    for copy in all_copies:
        copy.wait_send()
    pltpu.make_async_copy(arrived, arrived, all_send).wait()


def local(n, *arrays):
    anywhere = pl.BlockSpec(memory_space=pl.ANY)
    smem = pltpu.SMEM
    vmem = pltpu.VMEM
    dma = pltpu.SemaphoreType.DMA
    rhs = arrays[0]
    return pl.pallas_call(
        functools.partial(kernel, n),
        out_shape=pltpu.VMEM(rhs.shape, F32),
        in_specs=[anywhere] * 9,
        out_specs=pl.BlockSpec(memory_space=pltpu.VMEM),
        scratch_shapes=[
            smem((KL, TD), jnp.int32),
            smem((1, SLOTS), jnp.int32),
            smem((1, W), jnp.int32),
            vmem((SLOTS + PER_ROW * TD, WIDTH, WIDTH), BF16),
            vmem(rhs.shape, F32),
            vmem((ITERS + 1, TD, WIDTH), F32),
            vmem((ITERS - 1,) + rhs.shape, F32),
            vmem((TD, 2 * TD, WIDTH), BF16),
            vmem((TD * KL, 2 * TD, TILE), BF16),
            vmem((SLOTS, 1, TILE), jnp.int32),
            vmem((SLOTS * TILE, TILE), BF16),
            vmem((SLOTS, 2 * TD, TILE), BF16),
            vmem((ITERS, SLOTS, COMP, TILE), F32),
            vmem((ITERS, SLOTS, COMP, TILE), F32),
            vmem((n, TILE), F32),
            dma((6 + 2 * TD,)),
            dma((SLOTS,)),
            dma((SLOTS,)),
            dma((ITERS, SLOTS)),
            dma((ITERS, SLOTS)),
            pltpu.SemaphoreType.REGULAR((ITERS,)),
            dma,
            dma,
        ],
        compiler_params=pltpu.CompilerParams(
            collective_id=0, has_side_effects=True, vmem_limit_bytes=65_000_000
        ),
    )(*arrays[:5], arrays[5].T, arrays[6], jnp.swapaxes(arrays[7], 0, 1), arrays[8])


def solution(mesh):
    in_specs = (
        P(None, "parts"),
        P("parts", None, None),
        P("parts", None, None, None),
        P("parts", None, None),
        P("parts", None, None),
        P("parts", None),
        P("parts", None),
        P("parts", None, None),
        P("parts", None),
    )
    return jax.shard_map(
        functools.partial(local, mesh.shape["parts"]),
        mesh=mesh,
        in_specs=in_specs,
        out_specs=P(None, "parts"),
        check_vma=False,
    )
```

```python
import functools

import jax
import jax.numpy as jnp
from jax import lax
from jax.experimental import pallas as pl
from jax.experimental.pallas import tpu as pltpu
from jax.sharding import PartitionSpec as P

COMP = 4
TILE = 128
TD = 8
KL = 3
W = 3
ITERS = 3
WIDTH = COMP * TILE
SLOTS = 2 * W
PER_ROW = KL + 1
SHIFT = 2.0
EPS = 1e-06
LAG = 2
MESH = pl.DeviceIdType.MESH
F32 = jnp.float32
BF16 = jnp.bfloat16
SIDE = 4
LATE = {(i, ITERS): i for i in range(ITERS + 1)}
EARLY = {
    pair: TD + position
    for position, pair in enumerate((i, j) for i in range(ITERS) for j in range(i, ITERS))
}


def lanes(c):
    return slice(c * TILE, (c + 1) * TILE)


def halves(x):
    high = x.astype(BF16).astype(F32)
    return jnp.concatenate([high, x - high], axis=0).astype(BF16)


def small_solve(gram):
    n = ITERS + 1

    def g(i, j):
        return gram[(min(i, j), max(i, j))]

    def dot(u, v):
        total = None
        for i, a in u.items():
            for j, b in v.items():
                term = a * b * g(i, j)
                total = term if total is None else total + term
        return total

    beta = jnp.sqrt(g(0, 0) + EPS)
    basis = [{0: 1.0 / beta}]
    hess = {}
    for j in range(ITERS):
        w = {}
        for i, a in basis[j].items():
            w[i + 1] = a + w[i + 1] if i + 1 in w else a
            w[i] = SHIFT * a + w[i] if i in w else SHIFT * a
        for i in range(j + 1):
            hess[i, j] = dot(w, basis[i])
            for k, b in basis[i].items():
                w[k] = w[k] - hess[i, j] * b
        scale = jnp.sqrt(jnp.maximum(dot(w, w), 0.0) + EPS)
        hess[j + 1, j] = scale
        if j + 1 < ITERS:
            inverse = 1.0 / scale
            basis.append({k: a * inverse for k, a in w.items()})
    normal = {}
    for a in range(ITERS):
        for b in range(a + 1):
            normal[a, b] = sum(
                hess[i, a] * hess[i, b] for i in range(n) if (i, a) in hess and (i, b) in hess
            )
    target = [beta * hess[0, j] for j in range(ITERS)]
    low = {}
    inv = []
    for a in range(ITERS):
        for b in range(a):
            value = normal[a, b]
            for k in range(b):
                value = value - low[a, k] * low[b, k]
            low[a, b] = value * inv[b]
        value = normal[a, a]
        for k in range(a):
            value = value - low[a, k] * low[a, k]
        inv.append(1.0 / jnp.sqrt(value))
    inner = []
    for a in range(ITERS):
        value = target[a]
        for k in range(a):
            value = value - low[a, k] * inner[k]
        inner.append(value * inv[a])
    weights = [None] * ITERS
    for a in reversed(range(ITERS)):
        value = inner[a]
        for k in range(a + 1, ITERS):
            value = value - low[k, a] * weights[k]
        weights[a] = value * inv[a]
    out = []
    for i in range(ITERS):
        out.append(sum(weights[j] * basis[j][i] for j in range(ITERS) if i in basis[j]))
    return out


def kernel(
    n,
    rhs_hbm,
    diag_hbm,
    local_hbm,
    up_hbm,
    down_hbm,
    pattern_hbm,
    rows_hbm,
    ghost_hbm,
    live_hbm,
    out_ref,
    pattern,
    rows,
    live,
    tiles,
    rhs,
    krylov,
    nodes,
    spread,
    masks,
    ghosts,
    pick,
    place,
    sent,
    got,
    recv,
    load_sem,
    ghost_send,
    ghost_recv,
    halo_send,
    halo_recv,
    present,
    all_send,
    all_got,
):
    me = lax.axis_index("parts")
    around = [lax.rem(me + s + 1, n) for s in range(W)] + [
        lax.rem(me + n - s - 1, n) for s in range(W)
    ]
    core = lax.rem(me, 2)
    digits = [lax.rem(me // 2, SIDE), lax.rem(me // (2 * SIDE), SIDE), me // (2 * SIDE * SIDE)]
    moved = [
        [2 * SIDE**axis * lax.rem(digits[axis] + d, SIDE) for d in range(SIDE)] for axis in range(3)
    ]
    lines = [
        [me - moved[axis][0] + moved[axis][d] for d in range(1, SIDE)] for axis in range(3)
    ]
    greeted = around + lines[0] + lines[1] + lines[2]
    barrier = pltpu.get_barrier_semaphore()
    for other in greeted:
        pl.semaphore_signal(barrier, inc=1, device_id=(other,), device_id_type=MESH)
    partner = me + 1 - 2 * core

    loads = []

    def load(source, target):
        copy = pltpu.make_async_copy(source, target, load_sem.at[len(loads)])
        copy.start()
        loads.append(copy)
        return copy

    load_rhs = load(rhs_hbm, rhs)
    load_small = [load(rows_hbm, rows), load(live_hbm, live), load(pattern_hbm, pattern)]
    load_up = load(up_hbm, tiles.at[pl.ds(0, W)])
    load_down = load(down_hbm, tiles.at[pl.ds(W, W)])
    load_rows = []
    for t in range(TD):
        first = SLOTS + PER_ROW * t
        load_rows.append(
            (
                load(diag_hbm.at[t], tiles.at[first]),
                load(local_hbm.at[t], tiles.at[pl.ds(first + 1, KL)]),
            )
        )

    for copy in load_small:
        copy.wait()
    sub16 = lax.rem(lax.broadcasted_iota(jnp.int32, (2 * TD, TILE), 0), TD)
    sub8 = lax.broadcasted_iota(jnp.int32, (TD, TILE), 0)
    for t in range(TD):
        for k in range(KL):
            masks[KL * t + k] = jnp.where(sub16 == pattern[k, t], 1.0, 0.0).astype(BF16)

    load_rhs.wait()
    for t in range(TD):
        for c in range(COMP):
            krylov[0, t : t + 1, lanes(c)] = rhs[c : c + 1, lanes(t)]

    def spread_vector(j):
        for t in range(TD):
            row = jnp.broadcast_to(krylov[j, t : t + 1, :], (TD, WIDTH))
            spread[t] = halves(row)

    all_copies = []
    far = 1 - lax.rem(me, 2 * SIDE) // SIDE
    orders = []
    for side in range(2):
        down = far if side == 0 else 1 - far
        for k in reversed(range(W)):
            target = lax.rem(me + n + (k + 1) * (1 - 2 * down), n)
            orders.append((W * down + k, k, down, target))

    def product(order):
        s = order[0]
        return jnp.dot(spread[rows[0, s]], tiles[s], preferred_element_type=F32)

    def keep(j, order, both):
        s, k, down, target = order
        term = both[:TD] + both[TD:]
        message = term[:, lanes(0)]
        for c in range(1, COMP):
            message = jnp.where(sub8 == c, term[:, lanes(c)], message)
        factor = (down + (1 - down) * live[0, k]).astype(F32)
        sent[j, s] = (message * factor)[:COMP]

    def send(j, order):
        s, k, down, target = order
        copy = pltpu.make_async_remote_copy(
            src_ref=sent.at[j, s],
            dst_ref=got.at[j, s],
            send_sem=halo_send.at[j, s],
            recv_sem=halo_recv.at[j, s],
            device_id=(target,),
            device_id_type=MESH,
        )
        copy.start()
        all_copies.append(copy)

    def wait_halo(j):
        for s in range(SLOTS):
            pltpu.make_async_copy(got.at[j, s], got.at[j, s], halo_recv.at[j, s]).wait()

    def multiply_own(j):
        total = None
        for t in range(TD):
            if j == 0:
                for copy in load_rows[t]:
                    copy.wait()
            vector = spread[t]
            for k in range(PER_ROW):
                if k == 0:
                    mask = jnp.where(sub16 == t, 1.0, 0.0).astype(BF16)
                else:
                    mask = masks[KL * t + k - 1]
                left = vector * jnp.concatenate([mask] * COMP, axis=1)
                part = jnp.dot(left, tiles[SLOTS + PER_ROW * t + k], preferred_element_type=F32)
                total = part if total is None else total + part
        return total[:TD] + total[TD:]

    def finish(j, own):
        wait_halo(j)
        left = []
        for c in range(COMP):
            blocks = []
            for s in range(SLOTS):
                row = jnp.broadcast_to(got[j, s, c : c + 1, :], (TD, TILE))
                blocks.append(halves(row) * place[s])
            left.append(jnp.concatenate(blocks, axis=1))
        added = jnp.dot(jnp.concatenate(left, axis=0), pick[...], preferred_element_type=F32)
        for c in range(COMP):
            first = 2 * TD * c
            krylov[j + 1, :, lanes(c)] = (
                own[:, lanes(c)]
                + (added[first : first + TD] + added[first + TD : first + 2 * TD])
                - SHIFT * krylov[j, :, lanes(c)]
            )

    def pair_lanes(i, j):
        total = None
        for c in range(COMP):
            term = krylov[i, :, lanes(c)] * krylov[j, :, lanes(c)]
            total = term if total is None else total + term
        return jnp.sum(total, axis=1, keepdims=True)

    lane8 = lax.broadcasted_iota(jnp.int32, (TD, TILE), 1)

    def gather_pairs(pairs):
        total = jnp.zeros((TD, TILE), F32)
        for (i, j), position in pairs.items():
            total = jnp.where(lane8 == position, pair_lanes(i, j), total)
        return jnp.sum(total, axis=0, keepdims=True)

    for j in range(ITERS):
        spread_vector(j)
        if j == 0:
            load_up.wait()
            load_down.wait()
            found = [product(order) for order in orders]
            for order, both in zip(orders, found):
                keep(j, order, both)
            pl.semaphore_wait(barrier, len(greeted))
            for order in orders:
                send(j, order)
            for s, k, down, target in orders:
                copy = pltpu.make_async_remote_copy(
                    src_ref=ghost_hbm.at[s],
                    dst_ref=ghosts.at[s],
                    send_sem=ghost_send.at[s],
                    recv_sem=ghost_recv.at[s],
                    device_id=(target,),
                    device_id_type=MESH,
                )
                copy.start()
                all_copies.append(copy)
        else:
            found = []
            for position in range(SLOTS + LAG):
                if position < SLOTS:
                    found.append(product(orders[position]))
                if position >= LAG:
                    keep(j, orders[position - LAG], found[position - LAG])
                    send(j, orders[position - LAG])
        others = [lines[1], lines[2], [partner]][j]
        for other in others:
            pl.semaphore_signal(
                present.at[j], inc=1, device_id=(other,), device_id_type=MESH
            )
        own = multiply_own(j)
        pl.semaphore_wait(present.at[j], len(others))
        if j == 0:
            sub = lax.broadcasted_iota(jnp.int32, (TILE, TILE), 0)
            for s, k, down, target in orders:
                pltpu.make_async_copy(ghosts.at[s], ghosts.at[s], ghost_recv.at[s]).wait()
                index = jnp.broadcast_to(ghosts[s], (TILE, TILE))
                hit = jnp.where(jnp.bitwise_and(index, TILE - 1) == sub, 1.0, 0.0)
                pick[pl.ds(pl.multiple_of(s * TILE, TILE), TILE), :] = hit.T.astype(BF16)
                row = jnp.broadcast_to(ghosts[s], (2 * TD, TILE))
                hit = jnp.where(jnp.right_shift(row, 7) == sub16, 1.0, 0.0)
                place[s] = (hit * (1 - down + down * live[0, k]).astype(F32)).astype(BF16)
        if j + 1 == ITERS:
            early = gather_pairs(EARLY)
        finish(j, own)
    mine = early + gather_pairs(LATE)
    recv[pl.ds(me, 1), :] = mine
    for d in range(n - 1):
        target = d + jnp.minimum(jnp.maximum(d + 1 - me, 0), 1)
        pltpu.make_async_remote_copy(
            src_ref=recv.at[pl.ds(me, 1)],
            dst_ref=recv.at[pl.ds(me, 1)],
            send_sem=all_send,
            recv_sem=all_got,
            device_id=(target,),
            device_id_type=MESH,
        ).start()
    for j in range(1, ITERS):
        for t in range(TD):
            for c in range(COMP):
                nodes[j - 1, c : c + 1, lanes(t)] = krylov[j, t : t + 1, lanes(c)]
    arrived = recv.at[pl.ds(0, n - 1)]
    pltpu.make_async_copy(arrived, arrived, all_got).wait()
    sums = jnp.sum(recv[...], axis=0, keepdims=True)
    gram = {
        pair: jnp.broadcast_to(sums[:, position : position + 1], (TD, TILE))
        for pair, position in (EARLY | LATE).items()
    }
    weights = [weight[:COMP] for weight in small_solve(gram)]
    for t in range(TD):
        value = weights[0] * rhs[:, lanes(t)]
        for j in range(1, ITERS):
            value = value + weights[j] * nodes[j - 1, :, lanes(t)]
        out_ref[:, lanes(t)] = value
    for copy in all_copies:
        copy.wait_send()
    pltpu.make_async_copy(arrived, arrived, all_send).wait()


def local(n, *arrays):
    anywhere = pl.BlockSpec(memory_space=pl.ANY)
    smem = pltpu.SMEM
    vmem = pltpu.VMEM
    dma = pltpu.SemaphoreType.DMA
    rhs = arrays[0]
    return pl.pallas_call(
        functools.partial(kernel, n),
        out_shape=pltpu.VMEM(rhs.shape, F32),
        in_specs=[anywhere] * 9,
        out_specs=pl.BlockSpec(memory_space=pltpu.VMEM),
        scratch_shapes=[
            smem((KL, TD), jnp.int32),
            smem((1, SLOTS), jnp.int32),
            smem((1, W), jnp.int32),
            vmem((SLOTS + PER_ROW * TD, WIDTH, WIDTH), BF16),
            vmem(rhs.shape, F32),
            vmem((ITERS + 1, TD, WIDTH), F32),
            vmem((ITERS - 1,) + rhs.shape, F32),
            vmem((TD, 2 * TD, WIDTH), BF16),
            vmem((TD * KL, 2 * TD, TILE), BF16),
            vmem((SLOTS, 1, TILE), jnp.int32),
            vmem((SLOTS * TILE, TILE), BF16),
            vmem((SLOTS, 2 * TD, TILE), BF16),
            vmem((ITERS, SLOTS, COMP, TILE), F32),
            vmem((ITERS, SLOTS, COMP, TILE), F32),
            vmem((n, TILE), F32),
            dma((6 + 2 * TD,)),
            dma((SLOTS,)),
            dma((SLOTS,)),
            dma((ITERS, SLOTS)),
            dma((ITERS, SLOTS)),
            pltpu.SemaphoreType.REGULAR((ITERS,)),
            dma,
            dma,
        ],
        compiler_params=pltpu.CompilerParams(
            collective_id=0, has_side_effects=True, vmem_limit_bytes=65_000_000
        ),
    )(*arrays[:5], arrays[5].T, arrays[6], jnp.swapaxes(arrays[7], 0, 1), arrays[8])


def solution(mesh):
    in_specs = (
        P(None, "parts"),
        P("parts", None, None),
        P("parts", None, None, None),
        P("parts", None, None),
        P("parts", None, None),
        P("parts", None),
        P("parts", None),
        P("parts", None, None),
        P("parts", None),
    )
    return jax.shard_map(
        functools.partial(local, mesh.shape["parts"]),
        mesh=mesh,
        in_specs=in_specs,
        out_specs=P(None, "parts"),
        check_vma=False,
    )
```
